32 devices in a mesh: groups: 2 (over y), scen: 4 (over x, core), area: 4 (over z).
Axes of the slice: x: 2, y: 2, z: 4, core: 2. Of those that a mesh axis runs over, the one named last changes fastest.
Arguments:
- optimality_matrix_inverse: bfloat16 [8, 1024, 1024], P(('groups', 'area')), parts along dimension 0, as said below
- mean_requirement: bfloat16 [8, 1024, 16], P(('groups', 'area')), parts along dimension 0, may hold values from -6 to 6
- outcome_spread: bfloat16 [8, 1024, 2048], P(('groups', 'area'), None, 'scen'), parts along dimension 0, may hold values from -4 to 4
- outcome_likelihood_raw: float32 [256], P(('groups', 'scen')), parts along dimension 0, as said below
- prior_frontier_node_entries: bfloat16 [8, 32, 2048], P(('groups', 'area'), None, 'scen'), parts along dimension 0, may hold values from -6 to 6
- adjacent_regions: int32 [8, 4], P(('groups', 'area')), parts along dimension 0, may hold values from 0 to 3, as said below
- active_adjacent_entries: int32 [8], P(('groups', 'area')), parts along dimension 0, may hold values from 1 to 4
- linkage_entry_factor: float32 [8, 4], P(('groups', 'area')), parts along dimension 0, may hold values from 0.2 to 0.6
- plants_within_region: int32 [8], P(('groups', 'area')), parts along dimension 0, may hold values from 64 to 128
- inner_nodes_within_region: int32 [8], P(('groups', 'area')), parts along dimension 0, may hold values from 432 to 864
Outputs:
- commitment: float32 [8, 128, 16], P(('groups', 'area')), parts along dimension 0
- dual: float32 [8, 128, 2048], P(('groups', 'area'), None, 'scen'), parts along dimension 0
- boundary: float32 [8, 32, 2048], P(('groups', 'area'), None, 'scen'), parts along dimension 0
The draws below stay inside these ranges and needn't reach their ends.
There are 2 independent parts, one for each index of `groups`. The reference program is written for one: setup_inputs(seed, part) draws one part's arguments, and reference() takes and returns one part's arrays. A program takes and returns all parts, laid end to end along the dimension named above; each array names one. Nothing has to cross between parts.
Inputs may be any that keep to these rules, and one draw needn't show every extreme that they name: `adjacent_regions`: each area's neighbours are other areas, never itself. `optimality_matrix_inverse`: each area's matrix has a positive diagonal. `outcome_likelihood_raw`: positive weights.
All inputs are finite; a program needn't handle non-finite values.
Results may differ from the reference program's by a relative error of at most 0.01.
Values may be sent and summed in bfloat16 or wider, within the bound.
A program may use at most 64 MiB of HBM per device.

```python
import math
import jax
import jax.numpy as jnp
from jax import lax

OPTIMALITY_DIM = 1024
GEN = 128
BND = 32
NBUS = 864
PLANNING_SPAN = 16
MAXN = 4
ITERS = 2
OUTCOME_NUMBER = 128
REGION_NUMBER = 4


def draw_optimality_matrix_inverse(key, part):
    key_diag = jax.random.fold_in(key, 11)
    key_off = jax.random.fold_in(key, 12)
    diag = jnp.exp(jax.random.uniform(key_diag, (REGION_NUMBER, OPTIMALITY_DIM), jnp.float32, jnp.log(0.5), 0.0))
    off = 0.35 * jax.random.normal(key_off, (REGION_NUMBER, OPTIMALITY_DIM, OPTIMALITY_DIM), jnp.float32) / jnp.sqrt(jnp.float32(OPTIMALITY_DIM))
    eye = jnp.eye(OPTIMALITY_DIM, dtype=jnp.float32)
    return (off * (1.0 - eye)[None] + eye[None] * diag[:, :, None]).astype(jnp.bfloat16)


def draw_outcome_likelihood_raw(key, part):
    index = jnp.arange(OUTCOME_NUMBER, dtype=jnp.float32)
    place = index / jnp.float32(OUTCOME_NUMBER - 1)
    ramp = jnp.exp(place * jnp.log(jnp.float32(10.0)))
    factor = jnp.exp(jax.random.uniform(jax.random.fold_in(key, 21), (OUTCOME_NUMBER,), jnp.float32, -0.35, 0.35))
    return ramp * factor


def draw_adjacent_regions(key, part):
    offset = jax.random.randint(jax.random.fold_in(key, 31), (REGION_NUMBER, MAXN), 1, REGION_NUMBER)
    return ((jnp.arange(REGION_NUMBER, dtype=jnp.int32)[:, None] + offset) % REGION_NUMBER).astype(jnp.int32)


def set_ends(values, key, least, high):
    longest = values.shape.index(max(values.shape))
    spots = []
    for shift in (0, 1):
        where = [jax.random.randint(jax.random.fold_in(key, axis), (), 0, length) for axis, length in enumerate(values.shape)]
        where[longest] = (where[longest] + shift) % values.shape[longest]
        spots.append(tuple(where))
    return values.at[spots[0]].set(least).at[spots[1]].set(high)


def block_scale(key, shape, shards, low, top_value):
    level = 1.0
    for axis_at, blocks in shards:
        draws = jax.random.uniform(jax.random.fold_in(jax.random.fold_in(key, 6), axis_at), (blocks,), jnp.float32, low / len(shards), top_value / len(shards))
        level = level * jnp.repeat(jnp.exp(draws), shape[axis_at] // blocks).reshape((-1,) + (1,) * (len(shape) - 1 - axis_at))
    return level


def noise(stream_key, dims, scale, reach, split=(), kind=jnp.bfloat16):
    array = jax.random.normal(stream_key, dims, jnp.float32) * scale
    if len(split) > 0:
        array = block_scale(stream_key, dims, split, -0.22, 0.18) * array
    return jnp.clip(array, min=-reach, max=reach).astype(kind)


def setup_inputs(seed: int = 0, part: int = 0) -> dict:
    arg_keys = jax.random.split(jax.random.key(seed), 11)
    own_keys = jax.random.split(jax.random.fold_in(arg_keys[10], part), 11)
    optimality_matrix_inverse = draw_optimality_matrix_inverse(jax.random.fold_in(jax.random.fold_in(arg_keys[10], part), 71), part)
    mean_requirement = noise(own_keys[1], (REGION_NUMBER, OPTIMALITY_DIM, PLANNING_SPAN), 1.0, 6.0, ((0, 4),))
    outcome_spread = noise(own_keys[2], (REGION_NUMBER, OPTIMALITY_DIM, OUTCOME_NUMBER * PLANNING_SPAN), 0.5, 4.0, ((0, 4), (2, 4)))
    outcome_likelihood_raw = draw_outcome_likelihood_raw(jax.random.fold_in(jax.random.fold_in(arg_keys[10], part), 71), part)
    prior_frontier_node_entries = noise(own_keys[4], (REGION_NUMBER, BND, OUTCOME_NUMBER * PLANNING_SPAN), 1.0, 6.0, ((0, 4), (2, 4)))
    adjacent_regions = draw_adjacent_regions(jax.random.fold_in(jax.random.fold_in(arg_keys[10], part), 71), part)
    active_adjacent_entries = set_ends(jax.random.randint(own_keys[6], (REGION_NUMBER,), 1, MAXN + 1), jax.random.fold_in(own_keys[6], 1), 1, MAXN).astype(jnp.int32)
    linkage_entry_factor = jnp.clip(jnp.exp(math.log(0.6) - 1.0986123 * jax.random.uniform(own_keys[7], (REGION_NUMBER, MAXN), jnp.float32) ** block_scale(own_keys[7], (REGION_NUMBER, MAXN), ((0, 4),), -0.2, 0.2)), 0.2, 0.6)
    plants_within_region = set_ends(jax.random.randint(own_keys[8], (REGION_NUMBER,), GEN // 2, GEN + 1), jax.random.fold_in(own_keys[8], 1), GEN // 2, GEN).astype(jnp.int32)
    inner_nodes_within_region = set_ends(jax.random.randint(own_keys[9], (REGION_NUMBER,), NBUS // 2, NBUS + 1), jax.random.fold_in(own_keys[9], 1), NBUS // 2, NBUS).astype(jnp.int32)
    return dict(optimality_matrix_inverse=optimality_matrix_inverse, mean_requirement=mean_requirement, outcome_spread=outcome_spread, outcome_likelihood_raw=outcome_likelihood_raw, prior_frontier_node_entries=prior_frontier_node_entries, adjacent_regions=adjacent_regions, active_adjacent_entries=active_adjacent_entries, linkage_entry_factor=linkage_entry_factor, plants_within_region=plants_within_region, inner_nodes_within_region=inner_nodes_within_region)


penalty = 1.0


def reference(optimality_matrix_inverse, mean_requirement, outcome_spread, outcome_likelihood_raw, prior_frontier_node_entries, adjacent_regions, active_adjacent_entries, linkage_entry_factor, plants_within_region, inner_nodes_within_region):
    slots = jnp.arange(MAXN, dtype=jnp.int32)
    live = jnp.where(slots[None, :] < active_adjacent_entries[:, None], linkage_entry_factor, 0.0).astype(jnp.float32)
    onehot = (adjacent_regions[:, :, None] == jnp.arange(REGION_NUMBER, dtype=jnp.int32)[None, None, :]).astype(jnp.float32)
    adjacency = jnp.einsum('aj,ajb->ab', live, onehot)
    rows = jnp.arange(OPTIMALITY_DIM, dtype=jnp.int32)[None, :]
    inner = (rows >= GEN) & (rows < OPTIMALITY_DIM - BND)
    keep = jnp.where(inner & (rows - GEN >= inner_nodes_within_region[:, None]), 0.0, 1.0).astype(jnp.float32)
    consumer_requirement = mean_requirement.astype(jnp.float32)[:, :, None, :] + outcome_spread.astype(jnp.float32).reshape(REGION_NUMBER, OPTIMALITY_DIM, OUTCOME_NUMBER, PLANNING_SPAN)
    consumer_requirement = consumer_requirement * keep[:, :, None, None]
    prob = outcome_likelihood_raw / jnp.sum(outcome_likelihood_raw)
    gen_mask = (jnp.arange(GEN, dtype=jnp.int32)[None, :] < plants_within_region[:, None]).astype(jnp.float32)
    commitment = jnp.zeros((REGION_NUMBER, GEN, PLANNING_SPAN), jnp.float32)
    dual = jnp.zeros((REGION_NUMBER, GEN, OUTCOME_NUMBER, PLANNING_SPAN), jnp.float32)
    bound = prior_frontier_node_entries
    boundary = None
    for step in range(ITERS):
        tie = jnp.einsum('ab,bkc->akc', adjacency, bound.astype(jnp.float32)).reshape(REGION_NUMBER, BND, OUTCOME_NUMBER, PLANNING_SPAN)
        gen_part = consumer_requirement[:, :GEN] + penalty * (commitment[:, :, None, :] - dual)
        bnd_part = consumer_requirement[:, OPTIMALITY_DIM - BND:] + tie
        rhs = jnp.concatenate([gen_part, consumer_requirement[:, GEN:OPTIMALITY_DIM - BND], bnd_part], axis=1)
        rhs = rhs.astype(jnp.bfloat16).reshape(REGION_NUMBER, OPTIMALITY_DIM, OUTCOME_NUMBER * PLANNING_SPAN)
        state = lax.map(lambda pair: jnp.dot(pair[0], pair[1], preferred_element_type=jnp.float32), (optimality_matrix_inverse, rhs))
        commit = state[:, :GEN].reshape(REGION_NUMBER, GEN, OUTCOME_NUMBER, PLANNING_SPAN)
        avg = jnp.einsum('agsh,s->agh', commit, prob)
        commitment = jnp.clip(avg, 0.0, 1.0) * gen_mask[:, :, None]
        dual = dual + commit - commitment[:, :, None, :]
        boundary = state[:, OPTIMALITY_DIM - BND:]
        bound = boundary.astype(jnp.bfloat16)
    return commitment, dual.reshape(REGION_NUMBER, GEN, OUTCOME_NUMBER * PLANNING_SPAN), boundary
```

```python
import functools

import jax
import jax.numpy as jnp
from jax import lax
from jax.experimental import pallas as pl
from jax.experimental.pallas import tpu as pltpu
from jax.sharding import PartitionSpec as P

GEN = 128
BND = 32
MAXN = 4
LANES = 128
CHUNKS = 4
MESH = pl.DeviceIdType.MESH
F32 = jnp.float32
BF16 = jnp.bfloat16

penalty = 1.0


def dot(a, b):
    return jnp.dot(a, b, preferred_element_type=F32)


def halves(x, axis):
    high = x.astype(BF16)
    low = (x - high.astype(F32)).astype(BF16)
    return jnp.concatenate([high, low], axis=axis)


def kernel(
    n_area,
    n_scen,
    raw_hbm,
    near_hbm,
    live_hbm,
    gain_hbm,
    plants_hbm,
    inner_hbm,
    matrix_ref,
    mean_ref,
    spread_ref,
    prior_ref,
    commit_ref,
    dual_ref,
    bound_ref,
    raw_ref,
    near_ref,
    live_ref,
    gain_ref,
    plants_ref,
    inner_ref,
    rows_buf,
    mean_buf,
    spread_buf,
    prior_buf,
    couple_buf,
    base_buf,
    sums_buf,
    sums_in,
    small_buf,
    edge_in,
    load_sem,
    word_sem,
    send_sem,
    recv_sem,
    scen_send,
    scen_recv,
):
    order = matrix_ref.shape[2]
    columns = spread_ref.shape[2]
    hours = mean_ref.shape[1]
    scen_here = raw_ref.shape[0]
    rows = GEN + BND
    groups = LANES // hours
    depth = order // CHUNKS
    wide = n_area * BND
    me = lax.axis_index("area")
    scen = lax.axis_index("scen")

    barrier = pltpu.get_barrier_semaphore()
    for d in range(1, n_scen):
        pl.semaphore_signal(
            barrier, inc=1, device_id={"scen": lax.rem(scen + d, n_scen)}, device_id_type=MESH
        )
    for d in range(1, n_area):
        pl.semaphore_signal(
            barrier, inc=1, device_id={"area": lax.rem(me + d, n_area)}, device_id_type=MESH
        )

    others = [k + (k - me + n_area) // n_area for k in range(n_area - 1)]
    mine = pl.ds(pl.multiple_of(me * BND, BND), BND)
    my_small = pl.ds(pl.multiple_of(me * 8, 8), 8)
    loads = [
        pltpu.make_async_copy(prior_ref.at[0], prior_buf.at[mine], load_sem.at[0]),
        pltpu.make_async_copy(
            matrix_ref.at[0, pl.ds(0, GEN)], rows_buf.at[pl.ds(0, GEN)], load_sem.at[1]
        ),
        pltpu.make_async_copy(
            matrix_ref.at[0, pl.ds(order - BND, BND)], rows_buf.at[pl.ds(GEN, BND)], load_sem.at[2]
        ),
        pltpu.make_async_copy(mean_ref.at[0], mean_buf, load_sem.at[3]),
    ]
    for c in range(CHUNKS):
        part = pl.ds(c * depth, depth)
        loads.append(
            pltpu.make_async_copy(spread_ref.at[0, part], spread_buf.at[part], load_sem.at[4 + c])
        )
    pairs = (
        (raw_hbm, raw_ref),
        (near_hbm, near_ref),
        (live_hbm, live_ref),
        (gain_hbm, gain_ref),
        (plants_hbm, plants_ref),
        (inner_hbm, inner_ref),
    )
    words = [
        pltpu.make_async_copy(source, target, word_sem.at[i])
        for i, (source, target) in enumerate(pairs)
    ]
    for load in words + loads:
        load.start()

    def to_area(ref, rows_of, kind, area):
        own = rows_of(me)
        return pltpu.make_async_remote_copy(
            src_ref=ref.at[own],
            dst_ref=ref.at[own],
            send_sem=send_sem.at[kind, area],
            recv_sem=recv_sem.at[kind, me],
            device_id={"area": area},
            device_id_type=MESH,
        )

    def arrived(ref, rows_of, kind):
        for area in others:
            theirs = ref.at[rows_of(area)]
            pltpu.make_async_remote_copy(
                src_ref=theirs,
                dst_ref=theirs,
                send_sem=send_sem.at[kind, area],
                recv_sem=recv_sem.at[kind, area],
                device_id={"area": area},
                device_id_type=MESH,
            ).wait_recv()

    def tie_rows(area):
        return pl.ds(pl.multiple_of(area * BND, BND), BND)

    def small_rows(area):
        return pl.ds(pl.multiple_of(area * 8, 8), 8)

    kinds = ((prior_buf, tie_rows), (couple_buf, tie_rows), (base_buf, tie_rows))
    bulk = [[to_area(*pair, i, a) for i, pair in enumerate(kinds)] for a in others]
    send_small = [to_area(small_buf, small_rows, 3, a) for a in others]

    def to_scens(ref, target, kind):
        return [
            pltpu.make_async_remote_copy(
                src_ref=ref,
                dst_ref=target.at[d - 1],
                send_sem=scen_send.at[kind, d - 1],
                recv_sem=scen_recv.at[kind, d - 1],
                device_id={"scen": lax.rem(scen + d, n_scen)},
                device_id_type=MESH,
            )
            for d in range(1, n_scen)
        ]

    send_sums = to_scens(sums_buf, sums_in, 0)
    send_edge = to_scens(small_buf, edge_in, 1)

    for word in words:
        word.wait()
    loads[1].wait()
    loads[2].wait()
    pick_row = lax.broadcasted_iota(jnp.int32, (LANES, wide), 0)
    pick_col = lax.broadcasted_iota(jnp.int32, (LANES, wide), 1)
    pick = jnp.where(pick_row - (LANES - BND) == pick_col % BND, 1.0, 0.0).astype(BF16)
    area_of = lax.broadcasted_iota(jnp.int32, (1, wide), 1) // BND
    gain = jnp.zeros((1, wide), F32)
    for j in range(MAXN):
        factor = jnp.where(j < live_ref[0], gain_ref[0, j], 0.0)
        gain = gain + jnp.where(area_of == near_ref[0, j], factor, 0.0)
    couple = (dot(rows_buf[:, order - LANES :], pick) * gain).astype(BF16)
    couple_buf[mine, :] = couple[GEN:]

    place = lax.broadcasted_iota(jnp.int32, (1, order), 1)
    gone = (place >= GEN) & (place < order - BND) & (place - GEN >= inner_ref[0])
    keep = jnp.where(gone, 0.0, 1.0).astype(BF16)
    matrix = rows_buf[...] * keep
    lane = lax.broadcasted_iota(jnp.int32, (1, LANES), 1)
    hour_row = lax.broadcasted_iota(jnp.int32, (hours, LANES), 0)
    hour_col = lax.broadcasted_iota(jnp.int32, (hours, LANES), 1)
    same_hour = jnp.where(hour_row == hour_col % hours, 1.0, 0.0).astype(BF16)
    fold_row = lax.broadcasted_iota(jnp.int32, (LANES, LANES), 0)
    fold_col = lax.broadcasted_iota(jnp.int32, (LANES, LANES), 1)
    fold = jnp.where(fold_row % hours == fold_col % hours, 1.0, 0.0).astype(BF16)
    fold2 = jnp.concatenate([fold, fold], axis=0)
    loads[3].wait()
    level = lax.dot_general(
        matrix, mean_buf[...], (((1,), (1,)), ((), ())), preferred_element_type=F32
    )
    level = dot(halves(level, 1), jnp.concatenate([same_hour, same_hour], axis=0))
    state = jnp.concatenate([level] * (columns // LANES), axis=1)
    for c in range(CHUNKS):
        loads[4 + c].wait()
        state = state + dot(
            matrix[:, c * depth : (c + 1) * depth], spread_buf[pl.ds(c * depth, depth), :]
        )
    base_buf[mine, :] = state[GEN:].astype(BF16)

    scen_of = lax.broadcasted_iota(jnp.int32, (1, columns), 1) // hours
    weight = jnp.zeros((1, columns), F32)
    total = jnp.float32(0.0)
    for s in range(scen_here):
        weight = jnp.where(scen_of == s, raw_ref[s], weight)
        total = total + raw_ref[s]

    loads[0].wait()

    def squeeze(x):
        x = x * weight
        out = x[:, :LANES]
        for k in range(1, columns // LANES):
            out = out + x[:, k * LANES : (k + 1) * LANES]
        return out

    folded = jnp.concatenate([squeeze(state), squeeze(prior_buf[mine, :].astype(F32))], axis=0)
    folded = dot(halves(folded, 1), fold2)
    spot = [jnp.where(lane // hours == k, 1.0, 0.0) for k in range(groups)]

    def pack(x):
        step = x.shape[0] // groups
        out = x[:step] * spot[0]
        for k in range(1, groups):
            out = out + x[k * step : (k + 1) * step] * spot[k]
        return out

    gen_rows = GEN // groups
    sums = jnp.concatenate([pack(folded[:GEN]), jnp.full((8, LANES), total, F32)], axis=0)
    small_buf[my_small, :] = pack(folded[GEN:])
    sums_buf[...] = sums

    pl.semaphore_wait(barrier, n_area + n_scen - 2)
    for copy in send_small + send_sums + bulk[0]:
        copy.start()
    for copy in bulk[0]:
        copy.wait_send()
    for copy in sum(bulk[1:], []):
        copy.start()
    arrived(small_buf, small_rows, 3)
    for copy in send_edge:
        copy.start()

    arrived(prior_buf, tie_rows, 0)
    arrived(couple_buf, tie_rows, 1)
    prior = prior_buf[...]
    couples = couple_buf[...]
    first = state[:GEN] + dot(couple[:GEN], prior)
    edge = dot(couples, prior).astype(BF16)
    gen_part = matrix[:, :GEN]
    later = state - penalty * dot(gen_part, first.astype(BF16)) + dot(couple, edge)

    for copy in send_sums:
        copy.wait_recv()
    for d in range(1, n_scen):
        sums = sums + sums_in[d - 1]
    scale = 1.0 / sums[gen_rows:]
    means = sums[:gen_rows] * jnp.concatenate([scale] * (gen_rows // 8), axis=0)
    gen_mean = jnp.concatenate([means[:gen_rows] * spot[k] for k in range(groups)], axis=0)
    gen_mean = dot(halves(gen_mean, 1), fold2)
    for copy in send_edge:
        copy.wait_recv()
    small = small_buf[...]
    for d in range(1, n_scen):
        small = small + edge_in[d - 1]
    small = small * jnp.concatenate([scale] * n_area, axis=0)
    half = groups // 2
    edges = jnp.concatenate(
        [
            small[b * 8 : (b + 1) * 8] * spot[k + first_k]
            for first_k in (0, half)
            for b in range(n_area)
            for k in range(half)
        ],
        axis=0,
    )
    edges = dot(halves(edges, 1), fold2)
    prior_mean = edges[wide:].astype(BF16)
    edge_mean = (edges[:wide] + dot(couples, prior_mean)).astype(BF16)
    mean1 = gen_mean + dot(couple[:GEN], prior_mean)
    slot = lax.broadcasted_iota(jnp.int32, (GEN, LANES), 0)
    alive = jnp.where(slot < plants_ref[0], 1.0, 0.0)
    commit1 = jnp.clip(mean1, 0.0, 1.0) * alive
    both = jnp.concatenate([gen_part, gen_part], axis=1)
    mean2 = (
        gen_mean
        + penalty * dot(both[:GEN], halves(2.0 * commit1 - mean1, 0))
        + dot(couple[:GEN], edge_mean)
    )
    commit2 = jnp.clip(mean2, 0.0, 1.0) * alive
    push = dot(both, halves((2.0 * penalty) * commit1, 0))
    times = columns // LANES
    drop = jnp.concatenate([push[:GEN] - commit1 - commit2] * times, axis=1) + first
    commit_ref[0] = commit2.T[:hours]

    arrived(base_buf, tie_rows, 2)
    state2 = later + dot(couple, base_buf[...])
    dual_ref[0] = state2[:GEN] + drop
    bound_ref[0] = state2[GEN:] + jnp.concatenate([push[GEN:]] * times, axis=1)

    for copy in sum(bulk[1:], send_small + send_sums + send_edge):
        copy.wait_send()


def place(*refs):
    count = (len(refs) - 1) // 2
    sems = refs[-1]
    copies = [
        pltpu.make_async_copy(refs[i], refs[count + i], sems.at[i]) for i in range(count)
    ]
    for copy in copies:
        copy.start()
    for copy in copies:
        copy.wait()


def solution(mesh):
    n_area, n_scen = mesh.shape["area"], mesh.shape["scen"]

    def body(matrix, mean, spread, raw, prior, near, live, gain, plants, inner):
        order, columns, hours = matrix.shape[2], spread.shape[2], mean.shape[2]
        hbm = pl.BlockSpec(memory_space=pltpu.HBM)
        vmem = pl.BlockSpec(memory_space=pltpu.VMEM)
        rows = GEN + BND
        wide = n_area * BND
        packed = GEN * hours // LANES + 8
        results = pl.pallas_call(
            functools.partial(kernel, n_area, n_scen),
            out_shape=(
                pltpu.VMEM((1, hours, GEN), F32),
                pltpu.VMEM((1, GEN, columns), F32),
                pltpu.VMEM((1, BND, columns), F32),
            ),
            in_specs=[hbm] * 10,
            out_specs=(vmem,) * 3,
            scratch_shapes=[
                pltpu.SMEM(raw.shape, raw.dtype),
                pltpu.SMEM(near.shape, near.dtype),
                pltpu.SMEM(live.shape, live.dtype),
                pltpu.SMEM(gain.shape, gain.dtype),
                pltpu.SMEM(plants.shape, plants.dtype),
                pltpu.SMEM(inner.shape, inner.dtype),
                pltpu.VMEM((rows, order), BF16),
                pltpu.VMEM((hours, order), BF16),
                pltpu.VMEM((order, columns), BF16),
                pltpu.VMEM((wide, columns), BF16),
                pltpu.VMEM((wide, wide), BF16),
                pltpu.VMEM((wide, columns), BF16),
                pltpu.VMEM((packed, LANES), F32),
                pltpu.VMEM((n_scen - 1, packed, LANES), F32),
                pltpu.VMEM((n_area * 8, LANES), F32),
                pltpu.VMEM((n_scen - 1, n_area * 8, LANES), F32),
                pltpu.SemaphoreType.DMA((4 + CHUNKS,)),
                pltpu.SemaphoreType.DMA((6,)),
                pltpu.SemaphoreType.DMA((4, n_area)),
                pltpu.SemaphoreType.DMA((4, n_area)),
                pltpu.SemaphoreType.DMA((2, n_scen - 1)),
                pltpu.SemaphoreType.DMA((2, n_scen - 1)),
            ],
            compiler_params=pltpu.CompilerParams(
                collective_id=0, has_side_effects=True, vmem_limit_bytes=67043328 - 360 * 2**10
            ),
        )(
            raw,
            near,
            live,
            gain,
            plants,
            inner,
            matrix,
            jnp.swapaxes(mean, 1, 2),
            spread,
            prior,
        )
        commitment, dual, boundary = pl.pallas_call(
            place,
            out_shape=tuple(jax.ShapeDtypeStruct(x.shape, x.dtype) for x in results),
            in_specs=(vmem,) * 3,
            out_specs=(hbm,) * 3,
            scratch_shapes=[pltpu.SemaphoreType.DMA((3,))],
            compiler_params=pltpu.CompilerParams(vmem_limit_bytes=4 * 2**20),
        )(*results)
        return jnp.swapaxes(commitment, 1, 2), dual, boundary

    return jax.shard_map(
        body,
        mesh=mesh,
        in_specs=(
            P(("groups", "area"), None, None),
            P(("groups", "area"), None, None),
            P(("groups", "area"), None, "scen"),
            P(("groups", "scen")),
            P(("groups", "area"), None, "scen"),
            P(("groups", "area"), None),
            P(("groups", "area")),
            P(("groups", "area"), None),
            P(("groups", "area")),
            P(("groups", "area")),
        ),
        out_specs=(
            P(("groups", "area"), None, None),
            P(("groups", "area"), None, "scen"),
            P(("groups", "area"), None, "scen"),
        ),
        check_vma=False,
    )
```

```python
import functools

import jax
import jax.numpy as jnp
from jax import lax
from jax.experimental import pallas as pl
from jax.experimental.pallas import tpu as pltpu
from jax.sharding import PartitionSpec as P

GEN = 128
BND = 32
MAXN = 4
LANES = 128
CHUNKS = 1
MESH = pl.DeviceIdType.MESH
F32 = jnp.float32
BF16 = jnp.bfloat16

penalty = 1.0


def dot(a, b):
    return jnp.dot(a, b, preferred_element_type=F32)


def halves(x, axis):
    high = x.astype(BF16)
    low = (x - high.astype(F32)).astype(BF16)
    return jnp.concatenate([high, low], axis=axis)


def kernel(
    n_area,
    n_scen,
    raw_hbm,
    near_hbm,
    live_hbm,
    gain_hbm,
    plants_hbm,
    inner_hbm,
    matrix_ref,
    mean_ref,
    spread_ref,
    prior_ref,
    commit_ref,
    dual_ref,
    bound_ref,
    raw_ref,
    near_ref,
    live_ref,
    gain_ref,
    plants_ref,
    inner_ref,
    rows_buf,
    mean_buf,
    spread_buf,
    prior_buf,
    couple_buf,
    base_buf,
    sums_buf,
    sums_in,
    small_buf,
    edge_in,
    load_sem,
    word_sem,
    send_sem,
    recv_sem,
    scen_send,
    scen_recv,
):
    order = matrix_ref.shape[2]
    columns = spread_ref.shape[2]
    hours = mean_ref.shape[1]
    scen_here = raw_ref.shape[0]
    rows = GEN + BND
    groups = LANES // hours
    width = columns // CHUNKS
    wide = n_area * BND
    me = lax.axis_index("area")
    scen = lax.axis_index("scen")

    others = [k + (k - me + n_area) // n_area for k in range(n_area - 1)]
    mine = pl.ds(pl.multiple_of(me * BND, BND), BND)
    my_small = pl.ds(pl.multiple_of(me * 8, 8), 8)
    rows_in = [
        pltpu.make_async_copy(
            matrix_ref.at[0, pl.ds(0, GEN)], rows_buf.at[pl.ds(0, GEN)], load_sem.at[0]
        ),
        pltpu.make_async_copy(
            matrix_ref.at[0, pl.ds(order - BND, BND)], rows_buf.at[pl.ds(GEN, BND)], load_sem.at[1]
        ),
    ]
    mean_in = pltpu.make_async_copy(mean_ref.at[0], mean_buf, load_sem.at[2])
    prior_in = pltpu.make_async_copy(prior_ref.at[0], prior_buf.at[mine], load_sem.at[3])
    parts = [pl.ds(c * width, width) for c in range(CHUNKS)]
    spread_in = [
        pltpu.make_async_copy(
            spread_ref.at[0, :, part], spread_buf.at[:, part], load_sem.at[4 + c]
        )
        for c, part in enumerate(parts)
    ]
    pairs = (
        (raw_hbm, raw_ref),
        (near_hbm, near_ref),
        (live_hbm, live_ref),
        (gain_hbm, gain_ref),
        (plants_hbm, plants_ref),
        (inner_hbm, inner_ref),
    )
    words = [
        pltpu.make_async_copy(source, target, word_sem.at[i])
        for i, (source, target) in enumerate(pairs)
    ]
    for load in words + rows_in + [mean_in] + spread_in + [prior_in]:
        load.start()
    barrier = pltpu.get_barrier_semaphore()
    for d in range(1, n_scen):
        pl.semaphore_signal(
            barrier, inc=1, device_id={"scen": lax.rem(scen + d, n_scen)}, device_id_type=MESH
        )
    for d in range(1, n_area):
        pl.semaphore_signal(
            barrier, inc=1, device_id={"area": lax.rem(me + d, n_area)}, device_id_type=MESH
        )


    def to_area(ref, rows_of, kind, area):
        own = rows_of(me)
        return pltpu.make_async_remote_copy(
            src_ref=ref.at[own],
            dst_ref=ref.at[own],
            send_sem=send_sem.at[kind, area],
            recv_sem=recv_sem.at[kind, me],
            device_id={"area": area},
            device_id_type=MESH,
        )

    def arrived(ref, rows_of, kind):
        for area in others:
            theirs = ref.at[rows_of(area)]
            pltpu.make_async_remote_copy(
                src_ref=theirs,
                dst_ref=theirs,
                send_sem=send_sem.at[kind, area],
                recv_sem=recv_sem.at[kind, area],
                device_id={"area": area},
                device_id_type=MESH,
            ).wait_recv()

    def tie_rows(area):
        return pl.ds(pl.multiple_of(area * BND, BND), BND)

    def small_rows(area):
        return pl.ds(pl.multiple_of(area * 8, 8), 8)

    kinds = ((prior_buf, tie_rows), (couple_buf, tie_rows), (base_buf, tie_rows))
    bulk = [[to_area(*pair, i, a) for i, pair in enumerate(kinds)] for a in others]
    send_small = [to_area(small_buf, small_rows, 3, a) for a in others]

    def to_scens(ref, target, kind):
        return [
            pltpu.make_async_remote_copy(
                src_ref=ref,
                dst_ref=target.at[d - 1],
                send_sem=scen_send.at[kind, d - 1],
                recv_sem=scen_recv.at[kind, d - 1],
                device_id={"scen": lax.rem(scen + d, n_scen)},
                device_id_type=MESH,
            )
            for d in range(1, n_scen)
        ]

    send_sums = to_scens(sums_buf, sums_in, 0)
    send_edge = to_scens(small_buf, edge_in, 1)

    for word in words:
        word.wait()
    for load in rows_in:
        load.wait()
    pick_row = lax.broadcasted_iota(jnp.int32, (LANES, wide), 0)
    pick_col = lax.broadcasted_iota(jnp.int32, (LANES, wide), 1)
    pick = jnp.where(pick_row - (LANES - BND) == pick_col % BND, 1.0, 0.0).astype(BF16)
    area_of = lax.broadcasted_iota(jnp.int32, (1, wide), 1) // BND
    gain = jnp.zeros((1, wide), F32)
    for j in range(MAXN):
        factor = jnp.where(j < live_ref[0], gain_ref[0, j], 0.0)
        gain = gain + jnp.where(area_of == near_ref[0, j], factor, 0.0)
    couple = (dot(rows_buf[:, order - LANES :], pick) * gain).astype(BF16)
    couple_buf[mine, :] = couple[GEN:]

    place = lax.broadcasted_iota(jnp.int32, (1, order), 1)
    gone = (place >= GEN) & (place < order - BND) & (place - GEN >= inner_ref[0])
    keep = jnp.where(gone, 0.0, 1.0).astype(BF16)
    matrix = rows_buf[...] * keep
    lane = lax.broadcasted_iota(jnp.int32, (1, LANES), 1)
    hour_row = lax.broadcasted_iota(jnp.int32, (hours, LANES), 0)
    hour_col = lax.broadcasted_iota(jnp.int32, (hours, LANES), 1)
    same_hour = jnp.where(hour_row == hour_col % hours, 1.0, 0.0).astype(BF16)
    fold_row = lax.broadcasted_iota(jnp.int32, (LANES, LANES), 0)
    fold_col = lax.broadcasted_iota(jnp.int32, (LANES, LANES), 1)
    fold = jnp.where(fold_row % hours == fold_col % hours, 1.0, 0.0).astype(BF16)
    fold2 = jnp.concatenate([fold, fold], axis=0)
    mean_in.wait()
    level = lax.dot_general(
        matrix, mean_buf[...], (((1,), (1,)), ((), ())), preferred_element_type=F32
    )
    level = dot(halves(level, 1), jnp.concatenate([same_hour, same_hour], axis=0))
    states = []
    for load, part in zip(spread_in, parts):
        load.wait()
        states.append(
            dot(matrix, spread_buf[:, part]) + jnp.concatenate([level] * (width // LANES), axis=1)
        )
    state = jnp.concatenate(states, axis=1)
    base_buf[mine, :] = state[GEN:].astype(BF16)

    scen_of = lax.broadcasted_iota(jnp.int32, (1, columns), 1) // hours
    weight = jnp.zeros((1, columns), F32)
    total = jnp.float32(0.0)
    for s in range(scen_here):
        weight = jnp.where(scen_of == s, raw_ref[s], weight)
        total = total + raw_ref[s]

    prior_in.wait()

    def squeeze(x):
        x = x * weight
        out = x[:, :LANES]
        for k in range(1, columns // LANES):
            out = out + x[:, k * LANES : (k + 1) * LANES]
        return out

    folded = jnp.concatenate([squeeze(state), squeeze(prior_buf[mine, :].astype(F32))], axis=0)
    folded = dot(halves(folded, 1), fold2)
    spot = [jnp.where(lane // hours == k, 1.0, 0.0) for k in range(groups)]

    def pack(x):
        step = x.shape[0] // groups
        out = x[:step] * spot[0]
        for k in range(1, groups):
            out = out + x[k * step : (k + 1) * step] * spot[k]
        return out

    gen_rows = GEN // groups
    sums = jnp.concatenate([pack(folded[:GEN]), jnp.full((8, LANES), total, F32)], axis=0)
    small_buf[my_small, :] = pack(folded[GEN:])
    sums_buf[...] = sums

    pl.semaphore_wait(barrier, n_area + n_scen - 2)
    for copy in send_small + send_sums + bulk[0]:
        copy.start()
    for copy in bulk[0][:2]:
        copy.wait_send()
    for copy in sum(bulk[1:], []):
        copy.start()
    arrived(small_buf, small_rows, 3)
    for copy in send_edge:
        copy.start()

    arrived(prior_buf, tie_rows, 0)
    arrived(couple_buf, tie_rows, 1)
    prior = prior_buf[...]
    couples = couple_buf[...]
    first = state[:GEN] + dot(couple[:GEN], prior)
    edge = dot(couples, prior).astype(BF16)
    gen_part = matrix[:, :GEN]
    later = state - penalty * dot(gen_part, first.astype(BF16)) + dot(couple, edge)

    for copy in send_sums:
        copy.wait_recv()
    for d in range(1, n_scen):
        sums = sums + sums_in[d - 1]
    scale = 1.0 / sums[gen_rows:]
    means = sums[:gen_rows] * jnp.concatenate([scale] * (gen_rows // 8), axis=0)
    gen_mean = jnp.concatenate([means[:gen_rows] * spot[k] for k in range(groups)], axis=0)
    gen_mean = dot(halves(gen_mean, 1), fold2)
    for copy in send_edge:
        copy.wait_recv()
    small = small_buf[...]
    for d in range(1, n_scen):
        small = small + edge_in[d - 1]
    small = small * jnp.concatenate([scale] * n_area, axis=0)
    half = groups // 2
    edges = jnp.concatenate(
        [
            small[b * 8 : (b + 1) * 8] * spot[k + first_k]
            for first_k in (0, half)
            for b in range(n_area)
            for k in range(half)
        ],
        axis=0,
    )
    edges = dot(halves(edges, 1), fold2)
    prior_mean = edges[wide:].astype(BF16)
    edge_mean = (edges[:wide] + dot(couples, prior_mean)).astype(BF16)
    mean1 = gen_mean + dot(couple[:GEN], prior_mean)
    slot = lax.broadcasted_iota(jnp.int32, (GEN, LANES), 0)
    alive = jnp.where(slot < plants_ref[0], 1.0, 0.0)
    commit1 = jnp.clip(mean1, 0.0, 1.0) * alive
    both = jnp.concatenate([gen_part, gen_part], axis=1)
    mean2 = (
        gen_mean
        + penalty * dot(both[:GEN], halves(2.0 * commit1 - mean1, 0))
        + dot(couple[:GEN], edge_mean)
    )
    commit2 = jnp.clip(mean2, 0.0, 1.0) * alive
    push = dot(both, halves((2.0 * penalty) * commit1, 0))
    times = columns // LANES
    drop = jnp.concatenate([push[:GEN] - commit1 - commit2] * times, axis=1) + first
    commit_ref[0] = commit2.T[:hours]

    arrived(base_buf, tie_rows, 2)
    state2 = later + dot(couple, base_buf[...])
    dual_ref[0] = state2[:GEN] + drop
    bound_ref[0] = state2[GEN:] + jnp.concatenate([push[GEN:]] * times, axis=1)

    for copy in sum(bulk[1:], send_small + send_sums + send_edge + bulk[0][2:]):
        copy.wait_send()


def place(*refs):
    count = (len(refs) - 1) // 2
    sems = refs[-1]
    copies = [
        pltpu.make_async_copy(refs[i], refs[count + i], sems.at[i]) for i in range(count)
    ]
    for copy in copies:
        copy.start()
    for copy in copies:
        copy.wait()


def solution(mesh):
    n_area, n_scen = mesh.shape["area"], mesh.shape["scen"]

    def body(matrix, mean, spread, raw, prior, near, live, gain, plants, inner):
        order, columns, hours = matrix.shape[2], spread.shape[2], mean.shape[2]
        hbm = pl.BlockSpec(memory_space=pltpu.HBM)
        vmem = pl.BlockSpec(memory_space=pltpu.VMEM)
        rows = GEN + BND
        wide = n_area * BND
        packed = GEN * hours // LANES + 8
        results = pl.pallas_call(
            functools.partial(kernel, n_area, n_scen),
            out_shape=(
                pltpu.VMEM((1, hours, GEN), F32),
                pltpu.VMEM((1, GEN, columns), F32),
                pltpu.VMEM((1, BND, columns), F32),
            ),
            in_specs=[hbm] * 10,
            out_specs=(vmem,) * 3,
            scratch_shapes=[
                pltpu.SMEM(raw.shape, raw.dtype),
                pltpu.SMEM(near.shape, near.dtype),
                pltpu.SMEM(live.shape, live.dtype),
                pltpu.SMEM(gain.shape, gain.dtype),
                pltpu.SMEM(plants.shape, plants.dtype),
                pltpu.SMEM(inner.shape, inner.dtype),
                pltpu.VMEM((rows, order), BF16),
                pltpu.VMEM((hours, order), BF16),
                pltpu.VMEM((order, columns), BF16),
                pltpu.VMEM((wide, columns), BF16),
                pltpu.VMEM((wide, wide), BF16),
                pltpu.VMEM((wide, columns), BF16),
                pltpu.VMEM((packed, LANES), F32),
                pltpu.VMEM((n_scen - 1, packed, LANES), F32),
                pltpu.VMEM((n_area * 8, LANES), F32),
                pltpu.VMEM((n_scen - 1, n_area * 8, LANES), F32),
                pltpu.SemaphoreType.DMA((4 + CHUNKS,)),
                pltpu.SemaphoreType.DMA((6,)),
                pltpu.SemaphoreType.DMA((4, n_area)),
                pltpu.SemaphoreType.DMA((4, n_area)),
                pltpu.SemaphoreType.DMA((2, n_scen - 1)),
                pltpu.SemaphoreType.DMA((2, n_scen - 1)),
            ],
            compiler_params=pltpu.CompilerParams(
                collective_id=0, has_side_effects=True, vmem_limit_bytes=67043328 - 360 * 2**10
            ),
        )(
            raw,
            near,
            live,
            gain,
            plants,
            inner,
            matrix,
            jnp.swapaxes(mean, 1, 2),
            spread,
            prior,
        )
        commitment, dual, boundary = pl.pallas_call(
            place,
            out_shape=tuple(jax.ShapeDtypeStruct(x.shape, x.dtype) for x in results),
            in_specs=(vmem,) * 3,
            out_specs=(hbm,) * 3,
            scratch_shapes=[pltpu.SemaphoreType.DMA((3,))],
            compiler_params=pltpu.CompilerParams(vmem_limit_bytes=4 * 2**20),
        )(*results)
        return jnp.swapaxes(commitment, 1, 2), dual, boundary

    return jax.shard_map(
        body,
        mesh=mesh,
        in_specs=(
            P(("groups", "area"), None, None),
            P(("groups", "area"), None, None),
            P(("groups", "area"), None, "scen"),
            P(("groups", "scen")),
            P(("groups", "area"), None, "scen"),
            P(("groups", "area"), None),
            P(("groups", "area")),
            P(("groups", "area"), None),
            P(("groups", "area")),
            P(("groups", "area")),
        ),
        out_specs=(
            P(("groups", "area"), None, None),
            P(("groups", "area"), None, "scen"),
            P(("groups", "area"), None, "scen"),
        ),
        check_vma=False,
    )
```

```python
import functools

import jax
import jax.numpy as jnp
from jax import lax
from jax.experimental import pallas as pl
from jax.experimental.pallas import tpu as pltpu
from jax.sharding import PartitionSpec as P

GEN = 128
BND = 32
MAXN = 4
LANES = 128
CHUNKS = 1
EARLY = 2
MESH = pl.DeviceIdType.MESH
F32 = jnp.float32
BF16 = jnp.bfloat16

penalty = 1.0


def dot(a, b):
    return jnp.dot(a, b, preferred_element_type=F32)


def halves(x, axis):
    high = x.astype(BF16)
    low = (x - high.astype(F32)).astype(BF16)
    return jnp.concatenate([high, low], axis=axis)


def kernel(
    n_area,
    n_scen,
    raw_hbm,
    near_hbm,
    live_hbm,
    gain_hbm,
    plants_hbm,
    inner_hbm,
    matrix_ref,
    mean_ref,
    spread_ref,
    prior_ref,
    commit_ref,
    dual_ref,
    bound_ref,
    raw_ref,
    near_ref,
    live_ref,
    gain_ref,
    plants_ref,
    inner_ref,
    rows_buf,
    mean_buf,
    spread_buf,
    prior_buf,
    couple_buf,
    base_buf,
    sums_buf,
    sums_in,
    small_buf,
    edge_in,
    direct_buf,
    total_buf,
    load_sem,
    word_sem,
    send_sem,
    recv_sem,
    scen_send,
    scen_recv,
    direct_send,
    direct_recv,
    turn_sem,
):
    order = matrix_ref.shape[2]
    columns = spread_ref.shape[2]
    hours = mean_ref.shape[1]
    scen_here = raw_ref.shape[0]
    rows = GEN + BND
    groups = LANES // hours
    width = columns // CHUNKS
    wide = n_area * BND
    me = lax.axis_index("area")
    scen = lax.axis_index("scen")

    others = [k + (k - me + n_area) // n_area for k in range(n_area - 1)]
    mine = pl.ds(pl.multiple_of(me * BND, BND), BND)
    rows_in = [
        pltpu.make_async_copy(
            matrix_ref.at[0, pl.ds(0, GEN)], rows_buf.at[pl.ds(0, GEN)], load_sem.at[0]
        ),
        pltpu.make_async_copy(
            matrix_ref.at[0, pl.ds(order - BND, BND)], rows_buf.at[pl.ds(GEN, BND)], load_sem.at[1]
        ),
    ]
    mean_in = pltpu.make_async_copy(mean_ref.at[0], mean_buf, load_sem.at[2])
    prior_in = pltpu.make_async_copy(prior_ref.at[0], prior_buf.at[mine], load_sem.at[3])
    parts = [pl.ds(c * width, width) for c in range(CHUNKS)]
    spread_in = [
        pltpu.make_async_copy(
            spread_ref.at[0, :, part], spread_buf.at[:, part], load_sem.at[4 + c]
        )
        for c, part in enumerate(parts)
    ]
    pairs = (
        (raw_hbm, raw_ref),
        (near_hbm, near_ref),
        (live_hbm, live_ref),
        (gain_hbm, gain_ref),
        (plants_hbm, plants_ref),
        (inner_hbm, inner_ref),
    )
    words = [
        pltpu.make_async_copy(source, target, word_sem.at[i])
        for i, (source, target) in enumerate(pairs)
    ]
    for load in words + rows_in + [mean_in, prior_in] + spread_in:
        load.start()
    barrier = pltpu.get_barrier_semaphore()
    lead = (me == 0) & (scen < EARLY)

    @pl.when(lead)
    def _():
        for area in others:
            for d in range(1, n_scen):
                peer = {"area": area, "scen": lax.rem(scen + d, n_scen)}
                pl.semaphore_signal(barrier, inc=1, device_id=peer, device_id_type=MESH)

    for d in range(1, n_scen):
        pl.semaphore_signal(
            barrier, inc=1, device_id={"scen": lax.rem(scen + d, n_scen)}, device_id_type=MESH
        )
    for d in range(1, n_area):
        pl.semaphore_signal(
            barrier, inc=1, device_id={"area": lax.rem(me + d, n_area)}, device_id_type=MESH
        )


    def to_area(ref, rows_of, kind, area):
        own = rows_of(me)
        return pltpu.make_async_remote_copy(
            src_ref=ref.at[own],
            dst_ref=ref.at[own],
            send_sem=send_sem.at[kind, area],
            recv_sem=recv_sem.at[kind, me],
            device_id={"area": area},
            device_id_type=MESH,
        )

    def arrived(ref, rows_of, kind):
        for area in others:
            theirs = ref.at[rows_of(area)]
            pltpu.make_async_remote_copy(
                src_ref=theirs,
                dst_ref=theirs,
                send_sem=send_sem.at[kind, area],
                recv_sem=recv_sem.at[kind, area],
                device_id={"area": area},
                device_id_type=MESH,
            ).wait_recv()

    def tie_rows(area):
        return pl.ds(pl.multiple_of(area * BND, BND), BND)

    def small_rows(area):
        return area

    kinds = ((prior_buf, tie_rows), (couple_buf, tie_rows), (base_buf, tie_rows))
    bulk = [[to_area(*pair, i, a) for i, pair in enumerate(kinds)] for a in others]
    send_small = [to_area(small_buf, small_rows, 3, a) for a in others]

    def to_scens(ref, target, kind):
        return [
            pltpu.make_async_remote_copy(
                src_ref=ref,
                dst_ref=target.at[d - 1],
                send_sem=scen_send.at[kind, d - 1],
                recv_sem=scen_recv.at[kind, d - 1],
                device_id={"scen": lax.rem(scen + d, n_scen)},
                device_id_type=MESH,
            )
            for d in range(1, n_scen)
        ]

    send_sums = to_scens(sums_buf, sums_in, 0)
    send_edge = to_scens(small_buf, edge_in, 1)
    turns = [lax.rem(scen + d, n_scen) for d in range(n_scen)]

    def direct(target, area, source):
        return pltpu.make_async_remote_copy(
            src_ref=small_buf.at[me],
            dst_ref=direct_buf.at[area * n_scen + source],
            send_sem=direct_send.at[target],
            recv_sem=direct_recv.at[area * n_scen + source],
            device_id={"area": 0, "scen": target},
            device_id_type=MESH,
        )

    def send_direct(act):
        for target in range(EARLY):
            copy = direct(target, me, scen)

            @pl.when(scen != target)
            def _():
                act(copy)

    def send_edges(act):
        for d in range(1, n_scen):

            @pl.when((me > 0) | (turns[d] >= EARLY))
            def _():
                act(send_edge[d - 1])


    for word in words:
        word.wait()
    for load in rows_in:
        load.wait()
    pick_row = lax.broadcasted_iota(jnp.int32, (LANES, wide), 0)
    pick_col = lax.broadcasted_iota(jnp.int32, (LANES, wide), 1)
    pick = jnp.where(pick_row - (LANES - BND) == pick_col % BND, 1.0, 0.0).astype(BF16)
    area_of = lax.broadcasted_iota(jnp.int32, (1, wide), 1) // BND
    gain = jnp.zeros((1, wide), F32)
    for j in range(MAXN):
        factor = jnp.where(j < live_ref[0], gain_ref[0, j], 0.0)
        gain = gain + jnp.where(area_of == near_ref[0, j], factor, 0.0)
    couple = (dot(rows_buf[:, order - LANES :], pick) * gain).astype(BF16)
    couple_buf[mine, :] = couple[GEN:]

    place = lax.broadcasted_iota(jnp.int32, (1, order), 1)
    gone = (place >= GEN) & (place < order - BND) & (place - GEN >= inner_ref[0])
    keep = jnp.where(gone, 0.0, 1.0).astype(BF16)
    matrix = rows_buf[...] * keep
    lane = lax.broadcasted_iota(jnp.int32, (1, LANES), 1)
    hour_row = lax.broadcasted_iota(jnp.int32, (hours, LANES), 0)
    hour_col = lax.broadcasted_iota(jnp.int32, (hours, LANES), 1)
    same_hour = jnp.where(hour_row == hour_col % hours, 1.0, 0.0).astype(BF16)
    fold_row = lax.broadcasted_iota(jnp.int32, (LANES, LANES), 0)
    fold_col = lax.broadcasted_iota(jnp.int32, (LANES, LANES), 1)
    fold = jnp.where(fold_row % hours == fold_col % hours, 1.0, 0.0).astype(BF16)
    fold2 = jnp.concatenate([fold, fold], axis=0)
    mean_in.wait()
    level = lax.dot_general(
        matrix, mean_buf[...], (((1,), (1,)), ((), ())), preferred_element_type=F32
    )
    level = dot(halves(level, 1), jnp.concatenate([same_hour, same_hour], axis=0))
    scen_of = lax.broadcasted_iota(jnp.int32, (1, columns), 1) // hours
    weight = jnp.zeros((1, columns), F32)
    total = jnp.float32(0.0)
    for s in range(scen_here):
        weight = jnp.where(scen_of == s, raw_ref[s], weight)
        total = total + raw_ref[s]

    def squeeze(x):
        x = x * weight
        out = x[:, :LANES]
        for k in range(1, columns // LANES):
            out = out + x[:, k * LANES : (k + 1) * LANES]
        return out

    def pack(x):
        step = x.shape[0] // groups
        out = x[:step] * spot[0]
        for k in range(1, groups):
            out = out + x[k * step : (k + 1) * step] * spot[k]
        return out

    prior_in.wait()
    old = squeeze(prior_buf[mine, :].astype(F32))
    states = []
    for load, part in zip(spread_in, parts):
        load.wait()
        states.append(
            dot(matrix, spread_buf[:, part]) + jnp.concatenate([level] * (width // LANES), axis=1)
        )
    state = jnp.concatenate(states, axis=1)

    base_buf[mine, :] = state[GEN:].astype(BF16)
    far = (me + n_area - 1) // n_area
    late = (scen + n_scen - EARLY) // n_scen
    pl.semaphore_wait(barrier, n_area + n_scen - 2 + far * (EARLY - 1 + late))
    for some in bulk:
        some[1].start()
    spot = [jnp.where(lane // hours == k, 1.0, 0.0) for k in range(groups)]
    folded = jnp.concatenate([squeeze(state[GEN:]), old], axis=0)
    small_buf[me] = pack(dot(halves(folded, 1), fold2)).astype(BF16)

    send_direct(lambda copy: copy.start())
    for copy in send_small:
        copy.start()

    gen_rows = GEN // groups
    folded = dot(halves(squeeze(state[:GEN]), 1), fold2)
    sums = jnp.concatenate([pack(folded), jnp.full((8, LANES), total, F32)], axis=0)
    sums_buf[...] = sums
    for copy in send_sums:
        copy.start()
    odd = (me > 0) & (scen == 1)
    even = (me > 0) & (scen == 0)
    bulk[0][0].start()

    @pl.when(odd)
    def _():
        pl.semaphore_wait(turn_sem, 1)

    bulk[0][2].start()
    for k in range(1, n_area - 1):

        @pl.when(k >= me)
        def _():
            for copy in bulk[k][::2]:
                copy.start()

    for k in range(1, n_area - 1):

        @pl.when(k < me)
        def _():
            bulk[k][0].start()

    for copy in bulk[0][:2]:
        copy.wait_send()

    @pl.when(even)
    def _():
        pl.semaphore_signal(
            turn_sem, inc=1, device_id={"scen": scen + 1}, device_id_type=MESH
        )

    for k in range(1, n_area - 1):

        @pl.when(k < me)
        def _():
            bulk[k][2].start()

    arrived(small_buf, small_rows, 3)
    send_edges(lambda copy: copy.start())

    arrived(prior_buf, tie_rows, 0)
    arrived(couple_buf, tie_rows, 1)
    prior = prior_buf[...]
    couples = couple_buf[...]
    first = state[:GEN] + dot(couple[:GEN], prior)
    edge = dot(couples, prior).astype(BF16)
    gen_part = matrix[:, :GEN]
    later = state - penalty * dot(gen_part, first.astype(BF16)) + dot(couple, edge)

    for copy in send_sums:
        copy.wait_recv()
    for d in range(1, n_scen):
        sums = sums + sums_in[d - 1]
    scale = 1.0 / sums[gen_rows:]
    means = sums[:gen_rows] * jnp.concatenate([scale] * (gen_rows // 8), axis=0)
    gen_mean = jnp.concatenate([means[:gen_rows] * spot[k] for k in range(groups)], axis=0)
    gen_mean = dot(halves(gen_mean, 1), fold2)
    total_buf[...] = small_buf[...].astype(F32).reshape(total_buf.shape)

    @pl.when(lead)
    def _():
        for area in range(n_area):
            rows_of = slice(area * 8, (area + 1) * 8)
            for d in range(1, n_scen):
                direct(0, area, turns[d]).wait_recv()
                total_buf[rows_of] += direct_buf[area * n_scen + turns[d]].astype(F32)

    @pl.when(jnp.logical_not(lead))
    def _():
        for copy in send_edge:
            copy.wait_recv()
        for d in range(1, n_scen):
            total_buf[...] += edge_in[d - 1].astype(F32).reshape(total_buf.shape)

    small = total_buf[...]
    small = small * jnp.concatenate([scale] * n_area, axis=0)
    half = groups // 2
    edges = jnp.concatenate(
        [
            small[b * 8 : (b + 1) * 8] * spot[k + first_k]
            for first_k in (0, half)
            for b in range(n_area)
            for k in range(half)
        ],
        axis=0,
    )
    edges = dot(halves(edges, 1), fold2)
    prior_mean = edges[wide:].astype(BF16)
    edge_mean = (edges[:wide] + dot(couples, prior_mean)).astype(BF16)
    mean1 = gen_mean + dot(couple[:GEN], prior_mean)
    slot = lax.broadcasted_iota(jnp.int32, (GEN, LANES), 0)
    alive = jnp.where(slot < plants_ref[0], 1.0, 0.0)
    commit1 = jnp.clip(mean1, 0.0, 1.0) * alive
    both = jnp.concatenate([gen_part, gen_part], axis=1)
    mean2 = (
        gen_mean
        + penalty * dot(both[:GEN], halves(2.0 * commit1 - mean1, 0))
        + dot(couple[:GEN], edge_mean)
    )
    commit2 = jnp.clip(mean2, 0.0, 1.0) * alive
    push = dot(both, halves((2.0 * penalty) * commit1, 0))
    times = columns // LANES
    drop = jnp.concatenate([push[:GEN] - commit1 - commit2] * times, axis=1) + first
    commit_ref[0] = commit2.T[:hours]

    arrived(base_buf, tie_rows, 2)
    state2 = later + dot(couple, base_buf[...])
    dual_ref[0] = state2[:GEN] + drop
    bound_ref[0] = state2[GEN:] + jnp.concatenate([push[GEN:]] * times, axis=1)

    for copy in sum(bulk[1:], send_small + send_sums + bulk[0][2:]):
        copy.wait_send()
    send_direct(lambda copy: copy.wait_send())
    send_edges(lambda copy: copy.wait_send())


def place(*refs):
    count = (len(refs) - 1) // 2
    sems = refs[-1]
    copies = [
        pltpu.make_async_copy(refs[i], refs[count + i], sems.at[i]) for i in range(count)
    ]
    for copy in copies:
        copy.start()
    for copy in copies:
        copy.wait()


def solution(mesh):
    n_area, n_scen = mesh.shape["area"], mesh.shape["scen"]

    def body(matrix, mean, spread, raw, prior, near, live, gain, plants, inner):
        order, columns, hours = matrix.shape[2], spread.shape[2], mean.shape[2]
        hbm = pl.BlockSpec(memory_space=pltpu.HBM)
        vmem = pl.BlockSpec(memory_space=pltpu.VMEM)
        rows = GEN + BND
        wide = n_area * BND
        packed = GEN * hours // LANES + 8
        results = pl.pallas_call(
            functools.partial(kernel, n_area, n_scen),
            out_shape=(
                pltpu.VMEM((1, hours, GEN), F32),
                pltpu.VMEM((1, GEN, columns), F32),
                pltpu.VMEM((1, BND, columns), F32),
            ),
            in_specs=[hbm] * 10,
            out_specs=(vmem,) * 3,
            scratch_shapes=[
                pltpu.SMEM(raw.shape, raw.dtype),
                pltpu.SMEM(near.shape, near.dtype),
                pltpu.SMEM(live.shape, live.dtype),
                pltpu.SMEM(gain.shape, gain.dtype),
                pltpu.SMEM(plants.shape, plants.dtype),
                pltpu.SMEM(inner.shape, inner.dtype),
                pltpu.VMEM((rows, order), BF16),
                pltpu.VMEM((hours, order), BF16),
                pltpu.VMEM((order, columns), BF16),
                pltpu.VMEM((wide, columns), BF16),
                pltpu.VMEM((wide, wide), BF16),
                pltpu.VMEM((wide, columns), BF16),
                pltpu.VMEM((packed, LANES), F32),
                pltpu.VMEM((n_scen - 1, packed, LANES), F32),
                pltpu.VMEM((n_area, 8, LANES), BF16),
                pltpu.VMEM((n_scen - 1, n_area, 8, LANES), BF16),
                pltpu.VMEM((n_area * n_scen, 8, LANES), BF16),
                pltpu.VMEM((n_area * 8, LANES), F32),
                pltpu.SemaphoreType.DMA((4 + CHUNKS,)),
                pltpu.SemaphoreType.DMA((6,)),
                pltpu.SemaphoreType.DMA((4, n_area)),
                pltpu.SemaphoreType.DMA((4, n_area)),
                pltpu.SemaphoreType.DMA((2, n_scen - 1)),
                pltpu.SemaphoreType.DMA((2, n_scen - 1)),
                pltpu.SemaphoreType.DMA((EARLY,)),
                pltpu.SemaphoreType.DMA((n_area * n_scen,)),
                pltpu.SemaphoreType.REGULAR,
            ],
            compiler_params=pltpu.CompilerParams(
                collective_id=0, has_side_effects=True, vmem_limit_bytes=67043328 - 360 * 2**10
            ),
        )(
            raw,
            near,
            live,
            gain,
            plants,
            inner,
            matrix,
            jnp.swapaxes(mean, 1, 2),
            spread,
            prior,
        )
        commitment, dual, boundary = pl.pallas_call(
            place,
            out_shape=tuple(jax.ShapeDtypeStruct(x.shape, x.dtype) for x in results),
            in_specs=(vmem,) * 3,
            out_specs=(hbm,) * 3,
            scratch_shapes=[pltpu.SemaphoreType.DMA((3,))],
            compiler_params=pltpu.CompilerParams(vmem_limit_bytes=4 * 2**20),
        )(*results)
        return jnp.swapaxes(commitment, 1, 2), dual, boundary

    return jax.shard_map(
        body,
        mesh=mesh,
        in_specs=(
            P(("groups", "area"), None, None),
            P(("groups", "area"), None, None),
            P(("groups", "area"), None, "scen"),
            P(("groups", "scen")),
            P(("groups", "area"), None, "scen"),
            P(("groups", "area"), None),
            P(("groups", "area")),
            P(("groups", "area"), None),
            P(("groups", "area")),
            P(("groups", "area")),
        ),
        out_specs=(
            P(("groups", "area"), None, None),
            P(("groups", "area"), None, "scen"),
            P(("groups", "area"), None, "scen"),
        ),
        check_vma=False,
    )
```

```python
import functools

import jax
import jax.numpy as jnp
from jax import lax
from jax.experimental import pallas as pl
from jax.experimental.pallas import tpu as pltpu
from jax.sharding import PartitionSpec as P

GEN = 128
BND = 32
MAXN = 4
LANES = 128
CHUNKS = 1
EARLY = 2
MESH = pl.DeviceIdType.MESH
F32 = jnp.float32
BF16 = jnp.bfloat16

penalty = 1.0


def dot(a, b):
    return jnp.dot(a, b, preferred_element_type=F32)


def halves(x, axis):
    high = x.astype(BF16)
    low = (x - high.astype(F32)).astype(BF16)
    return jnp.concatenate([high, low], axis=axis)


def kernel(
    n_area,
    n_scen,
    raw_hbm,
    near_hbm,
    live_hbm,
    gain_hbm,
    plants_hbm,
    inner_hbm,
    matrix_ref,
    mean_ref,
    spread_ref,
    prior_ref,
    commit_ref,
    dual_ref,
    bound_ref,
    raw_ref,
    near_ref,
    live_ref,
    gain_ref,
    plants_ref,
    inner_ref,
    rows_buf,
    mean_buf,
    spread_buf,
    prior_buf,
    couple_buf,
    base_buf,
    sums_buf,
    sums_in,
    small_buf,
    edge_in,
    direct_buf,
    total_buf,
    load_sem,
    word_sem,
    send_sem,
    recv_sem,
    scen_send,
    scen_recv,
    direct_send,
    direct_recv,
    turn_sem,
):
    order = matrix_ref.shape[2]
    columns = spread_ref.shape[2]
    hours = mean_ref.shape[1]
    scen_here = raw_ref.shape[0]
    rows = GEN + BND
    groups = LANES // hours
    width = columns // CHUNKS
    wide = n_area * BND
    me = lax.axis_index("area")
    scen = lax.axis_index("scen")

    others = [k + (k - me + n_area) // n_area for k in range(n_area - 1)]
    mine = pl.ds(pl.multiple_of(me * BND, BND), BND)
    rows_in = [
        pltpu.make_async_copy(
            matrix_ref.at[0, pl.ds(0, GEN)], rows_buf.at[pl.ds(0, GEN)], load_sem.at[0]
        ),
        pltpu.make_async_copy(
            matrix_ref.at[0, pl.ds(order - BND, BND)], rows_buf.at[pl.ds(GEN, BND)], load_sem.at[1]
        ),
    ]
    mean_in = pltpu.make_async_copy(mean_ref.at[0], mean_buf, load_sem.at[2])
    prior_in = pltpu.make_async_copy(prior_ref.at[0], prior_buf.at[mine], load_sem.at[3])
    parts = [pl.ds(c * width, width) for c in range(CHUNKS)]
    spread_in = [
        pltpu.make_async_copy(
            spread_ref.at[0, :, part], spread_buf.at[:, part], load_sem.at[4 + c]
        )
        for c, part in enumerate(parts)
    ]
    pairs = (
        (raw_hbm, raw_ref),
        (near_hbm, near_ref),
        (live_hbm, live_ref),
        (gain_hbm, gain_ref),
        (plants_hbm, plants_ref),
        (inner_hbm, inner_ref),
    )
    words = [
        pltpu.make_async_copy(source, target, word_sem.at[i])
        for i, (source, target) in enumerate(pairs)
    ]
    for load in words + rows_in + [mean_in, prior_in] + spread_in:
        load.start()
    barrier = pltpu.get_barrier_semaphore()
    lead = (me == 0) & (scen < EARLY)

    @pl.when(lead)
    def _():
        for area in others:
            for d in range(1, n_scen):
                peer = {"area": area, "scen": lax.rem(scen + d, n_scen)}
                pl.semaphore_signal(barrier, inc=1, device_id=peer, device_id_type=MESH)

    for d in range(1, n_scen):
        pl.semaphore_signal(
            barrier, inc=1, device_id={"scen": lax.rem(scen + d, n_scen)}, device_id_type=MESH
        )
    for d in range(1, n_area):
        pl.semaphore_signal(
            barrier, inc=1, device_id={"area": lax.rem(me + d, n_area)}, device_id_type=MESH
        )


    def to_area(ref, rows_of, kind, area):
        own = rows_of(me)
        return pltpu.make_async_remote_copy(
            src_ref=ref.at[own],
            dst_ref=ref.at[own],
            send_sem=send_sem.at[kind, area],
            recv_sem=recv_sem.at[kind, me],
            device_id={"area": area},
            device_id_type=MESH,
        )

    def arrived(ref, rows_of, kind):
        for area in others:
            theirs = ref.at[rows_of(area)]
            pltpu.make_async_remote_copy(
                src_ref=theirs,
                dst_ref=theirs,
                send_sem=send_sem.at[kind, area],
                recv_sem=recv_sem.at[kind, area],
                device_id={"area": area},
                device_id_type=MESH,
            ).wait_recv()

    def tie_rows(area):
        return pl.ds(pl.multiple_of(area * BND, BND), BND)

    def small_rows(area):
        return area

    kinds = ((prior_buf, tie_rows), (couple_buf, small_rows), (base_buf, tie_rows))
    bulk = [[to_area(*pair, i, a) for i, pair in enumerate(kinds)] for a in others]
    send_small = [to_area(small_buf, small_rows, 3, a) for a in others]

    def to_scens(ref, target, kind):
        return [
            pltpu.make_async_remote_copy(
                src_ref=ref,
                dst_ref=target.at[d - 1],
                send_sem=scen_send.at[kind, d - 1],
                recv_sem=scen_recv.at[kind, d - 1],
                device_id={"scen": lax.rem(scen + d, n_scen)},
                device_id_type=MESH,
            )
            for d in range(1, n_scen)
        ]

    send_sums = to_scens(sums_buf, sums_in, 0)
    send_edge = to_scens(small_buf, edge_in, 1)
    turns = [lax.rem(scen + d, n_scen) for d in range(n_scen)]

    def direct(target, area, source):
        return pltpu.make_async_remote_copy(
            src_ref=small_buf.at[me],
            dst_ref=direct_buf.at[area * n_scen + source],
            send_sem=direct_send.at[target],
            recv_sem=direct_recv.at[area * n_scen + source],
            device_id={"area": 0, "scen": target},
            device_id_type=MESH,
        )

    def send_direct(act):
        for target in range(EARLY):
            copy = direct(target, me, scen)

            @pl.when(scen != target)
            def _():
                act(copy)

    def send_edges(act):
        for d in range(1, n_scen):

            @pl.when((me > 0) | (turns[d] >= EARLY))
            def _():
                act(send_edge[d - 1])


    for word in words:
        word.wait()
    for load in rows_in:
        load.wait()
    pick_row = lax.broadcasted_iota(jnp.int32, (LANES, wide), 0)
    pick_col = lax.broadcasted_iota(jnp.int32, (LANES, wide), 1)
    pick = jnp.where(pick_row - (LANES - BND) == pick_col % BND, 1.0, 0.0).astype(BF16)
    area_of = lax.broadcasted_iota(jnp.int32, (1, wide), 1) // BND
    gain = jnp.zeros((1, wide), F32)
    for j in range(MAXN):
        factor = jnp.where(j < live_ref[0], gain_ref[0, j], 0.0)
        gain = gain + jnp.where(area_of == near_ref[0, j], factor, 0.0)
    corner = dot(rows_buf[:, order - LANES :], pick)
    couple = (corner * gain).astype(BF16)
    eights = BND // 8
    high = gain.astype(BF16).astype(F32)
    part_row = lax.broadcasted_iota(jnp.int32, (8, wide), 0)
    thin = jnp.zeros((8, wide), F32)
    for q in range(eights):
        thin = thin + jnp.where(area_of == q, corner[GEN + q * 8 : GEN + q * 8 + 8], 0.0)
    gains = jnp.where(part_row < 4, high, gain - high)
    couple_buf[me] = jnp.concatenate([thin, gains], axis=0).astype(BF16)

    place = lax.broadcasted_iota(jnp.int32, (1, order), 1)
    gone = (place >= GEN) & (place < order - BND) & (place - GEN >= inner_ref[0])
    keep = jnp.where(gone, 0.0, 1.0).astype(BF16)
    matrix = rows_buf[...] * keep
    lane = lax.broadcasted_iota(jnp.int32, (1, LANES), 1)
    hour_row = lax.broadcasted_iota(jnp.int32, (hours, LANES), 0)
    hour_col = lax.broadcasted_iota(jnp.int32, (hours, LANES), 1)
    same_hour = jnp.where(hour_row == hour_col % hours, 1.0, 0.0).astype(BF16)
    fold_row = lax.broadcasted_iota(jnp.int32, (LANES, LANES), 0)
    fold_col = lax.broadcasted_iota(jnp.int32, (LANES, LANES), 1)
    fold = jnp.where(fold_row % hours == fold_col % hours, 1.0, 0.0).astype(BF16)
    fold2 = jnp.concatenate([fold, fold], axis=0)
    mean_in.wait()
    level = lax.dot_general(
        matrix, mean_buf[...], (((1,), (1,)), ((), ())), preferred_element_type=F32
    )
    level = dot(halves(level, 1), jnp.concatenate([same_hour, same_hour], axis=0))
    scen_of = lax.broadcasted_iota(jnp.int32, (1, columns), 1) // hours
    weight = jnp.zeros((1, columns), F32)
    total = jnp.float32(0.0)
    for s in range(scen_here):
        weight = jnp.where(scen_of == s, raw_ref[s], weight)
        total = total + raw_ref[s]

    def squeeze(x):
        x = x * weight
        out = x[:, :LANES]
        for k in range(1, columns // LANES):
            out = out + x[:, k * LANES : (k + 1) * LANES]
        return out

    def pack(x):
        step = x.shape[0] // groups
        out = x[:step] * spot[0]
        for k in range(1, groups):
            out = out + x[k * step : (k + 1) * step] * spot[k]
        return out

    prior_in.wait()
    old = squeeze(prior_buf[mine, :].astype(F32))
    states = []
    for load, part in zip(spread_in, parts):
        load.wait()
        states.append(
            dot(matrix, spread_buf[:, part]) + jnp.concatenate([level] * (width // LANES), axis=1)
        )
    state = jnp.concatenate(states, axis=1)

    base_buf[mine, :] = state[GEN:].astype(BF16)
    far = (me + n_area - 1) // n_area
    late = (scen + n_scen - EARLY) // n_scen
    pl.semaphore_wait(barrier, n_area + n_scen - 2 + far * (EARLY - 1 + late))
    for some in bulk:
        some[1].start()
    spot = [jnp.where(lane // hours == k, 1.0, 0.0) for k in range(groups)]
    folded = jnp.concatenate([squeeze(state[GEN:]), old], axis=0)
    small_buf[me] = pack(dot(halves(folded, 1), fold2)).astype(BF16)

    send_direct(lambda copy: copy.start())
    for copy in send_small:
        copy.start()

    gen_rows = GEN // groups
    folded = dot(halves(squeeze(state[:GEN]), 1), fold2)
    sums = jnp.concatenate([pack(folded), jnp.full((8, LANES), total, F32)], axis=0)
    sums_buf[...] = sums
    for copy in send_sums:
        copy.start()
    odd = (me > 0) & (scen == 1)
    even = (me > 0) & (scen == 0)
    bulk[0][0].start()

    @pl.when(jnp.logical_not(odd))
    def _():
        bulk[0][2].start()

    for k in range(1, n_area - 1):

        @pl.when(k >= me)
        def _():
            for copy in bulk[k][::2]:
                copy.start()

    for k in range(1, n_area - 1):

        @pl.when(k < me)
        def _():
            bulk[k][0].start()

    @pl.when(odd)
    def _():
        pl.semaphore_wait(turn_sem, 1)
        bulk[0][2].start()

    for copy in bulk[0][:2]:
        copy.wait_send()

    @pl.when(even)
    def _():
        pl.semaphore_signal(
            turn_sem, inc=1, device_id={"scen": scen + 1}, device_id_type=MESH
        )

    for k in range(1, n_area - 1):

        @pl.when(k < me)
        def _():
            bulk[k][2].start()

    arrived(small_buf, small_rows, 3)
    send_edges(lambda copy: copy.start())

    arrived(prior_buf, tie_rows, 0)
    arrived(couple_buf, small_rows, 1)
    prior = prior_buf[...]
    thin = couple_buf[...].astype(F32)
    slots = [jnp.where(lane // BND == q, 1.0, 0.0) for q in range(eights)]
    couples = jnp.concatenate(
        [thin[b, :8, :LANES] * slots[q] for b in range(n_area) for q in range(eights)], axis=0
    )
    tie_row = lax.broadcasted_iota(jnp.int32, (LANES, wide), 0)
    same_tie = jnp.where(tie_row % BND == pick_col % BND, 1.0, 0.0).astype(BF16)
    gains = jnp.concatenate(
        [jnp.broadcast_to(thin[b, 8:9] + thin[b, 12:13], (BND, wide)) for b in range(n_area)],
        axis=0,
    )
    couples = (dot(couples.astype(BF16), same_tie) * gains).astype(BF16)
    first = state[:GEN] + dot(couple[:GEN], prior)
    edge = dot(couples, prior).astype(BF16)
    gen_part = matrix[:, :GEN]
    later = state - penalty * dot(gen_part, first.astype(BF16)) + dot(couple, edge)

    for copy in send_sums:
        copy.wait_recv()
    for d in range(1, n_scen):
        sums = sums + sums_in[d - 1]
    scale = 1.0 / sums[gen_rows:]
    means = sums[:gen_rows] * jnp.concatenate([scale] * (gen_rows // 8), axis=0)
    gen_mean = jnp.concatenate([means[:gen_rows] * spot[k] for k in range(groups)], axis=0)
    gen_mean = dot(halves(gen_mean, 1), fold2)
    total_buf[...] = small_buf[...].astype(F32).reshape(total_buf.shape)

    @pl.when(lead)
    def _():
        for area in range(n_area):
            rows_of = slice(area * 8, (area + 1) * 8)
            for d in range(1, n_scen):
                direct(0, area, turns[d]).wait_recv()
                total_buf[rows_of] += direct_buf[area * n_scen + turns[d]].astype(F32)

    @pl.when(jnp.logical_not(lead))
    def _():
        for copy in send_edge:
            copy.wait_recv()
        for d in range(1, n_scen):
            total_buf[...] += edge_in[d - 1].astype(F32).reshape(total_buf.shape)

    small = total_buf[...]
    small = small * jnp.concatenate([scale] * n_area, axis=0)
    half = groups // 2
    edges = jnp.concatenate(
        [
            small[b * 8 : (b + 1) * 8] * spot[k + first_k]
            for first_k in (0, half)
            for b in range(n_area)
            for k in range(half)
        ],
        axis=0,
    )
    edges = dot(halves(edges, 1), fold2)
    prior_mean = edges[wide:].astype(BF16)
    edge_mean = (edges[:wide] + dot(couples, prior_mean)).astype(BF16)
    mean1 = gen_mean + dot(couple[:GEN], prior_mean)
    slot = lax.broadcasted_iota(jnp.int32, (GEN, LANES), 0)
    alive = jnp.where(slot < plants_ref[0], 1.0, 0.0)
    commit1 = jnp.clip(mean1, 0.0, 1.0) * alive
    both = jnp.concatenate([gen_part, gen_part], axis=1)
    mean2 = (
        gen_mean
        + penalty * dot(both[:GEN], halves(2.0 * commit1 - mean1, 0))
        + dot(couple[:GEN], edge_mean)
    )
    commit2 = jnp.clip(mean2, 0.0, 1.0) * alive
    push = dot(both, halves((2.0 * penalty) * commit1, 0))
    times = columns // LANES
    drop = jnp.concatenate([push[:GEN] - commit1 - commit2] * times, axis=1) + first
    commit_ref[0] = commit2.T[:hours]

    arrived(base_buf, tie_rows, 2)
    state2 = later + dot(couple, base_buf[...])
    dual_ref[0] = state2[:GEN] + drop
    bound_ref[0] = state2[GEN:] + jnp.concatenate([push[GEN:]] * times, axis=1)

    for copy in sum(bulk[1:], send_small + send_sums + bulk[0][2:]):
        copy.wait_send()
    send_direct(lambda copy: copy.wait_send())
    send_edges(lambda copy: copy.wait_send())


def place(*refs):
    count = (len(refs) - 1) // 2
    sems = refs[-1]
    copies = [
        pltpu.make_async_copy(refs[i], refs[count + i], sems.at[i]) for i in range(count)
    ]
    for copy in copies:
        copy.start()
    for copy in copies:
        copy.wait()


def solution(mesh):
    n_area, n_scen = mesh.shape["area"], mesh.shape["scen"]

    def body(matrix, mean, spread, raw, prior, near, live, gain, plants, inner):
        order, columns, hours = matrix.shape[2], spread.shape[2], mean.shape[2]
        hbm = pl.BlockSpec(memory_space=pltpu.HBM)
        vmem = pl.BlockSpec(memory_space=pltpu.VMEM)
        rows = GEN + BND
        wide = n_area * BND
        packed = GEN * hours // LANES + 8
        results = pl.pallas_call(
            functools.partial(kernel, n_area, n_scen),
            out_shape=(
                pltpu.VMEM((1, hours, GEN), F32),
                pltpu.VMEM((1, GEN, columns), F32),
                pltpu.VMEM((1, BND, columns), F32),
            ),
            in_specs=[hbm] * 10,
            out_specs=(vmem,) * 3,
            scratch_shapes=[
                pltpu.SMEM(raw.shape, raw.dtype),
                pltpu.SMEM(near.shape, near.dtype),
                pltpu.SMEM(live.shape, live.dtype),
                pltpu.SMEM(gain.shape, gain.dtype),
                pltpu.SMEM(plants.shape, plants.dtype),
                pltpu.SMEM(inner.shape, inner.dtype),
                pltpu.VMEM((rows, order), BF16),
                pltpu.VMEM((hours, order), BF16),
                pltpu.VMEM((order, columns), BF16),
                pltpu.VMEM((wide, columns), BF16),
                pltpu.VMEM((n_area, 16, wide), BF16),
                pltpu.VMEM((wide, columns), BF16),
                pltpu.VMEM((packed, LANES), F32),
                pltpu.VMEM((n_scen - 1, packed, LANES), F32),
                pltpu.VMEM((n_area, 8, LANES), BF16),
                pltpu.VMEM((n_scen - 1, n_area, 8, LANES), BF16),
                pltpu.VMEM((n_area * n_scen, 8, LANES), BF16),
                pltpu.VMEM((n_area * 8, LANES), F32),
                pltpu.SemaphoreType.DMA((4 + CHUNKS,)),
                pltpu.SemaphoreType.DMA((6,)),
                pltpu.SemaphoreType.DMA((4, n_area)),
                pltpu.SemaphoreType.DMA((4, n_area)),
                pltpu.SemaphoreType.DMA((2, n_scen - 1)),
                pltpu.SemaphoreType.DMA((2, n_scen - 1)),
                pltpu.SemaphoreType.DMA((EARLY,)),
                pltpu.SemaphoreType.DMA((n_area * n_scen,)),
                pltpu.SemaphoreType.REGULAR,
            ],
            compiler_params=pltpu.CompilerParams(
                collective_id=0, has_side_effects=True, vmem_limit_bytes=67043328 - 360 * 2**10
            ),
        )(
            raw,
            near,
            live,
            gain,
            plants,
            inner,
            matrix,
            jnp.swapaxes(mean, 1, 2),
            spread,
            prior,
        )
        commitment, dual, boundary = pl.pallas_call(
            place,
            out_shape=tuple(jax.ShapeDtypeStruct(x.shape, x.dtype) for x in results),
            in_specs=(vmem,) * 3,
            out_specs=(hbm,) * 3,
            scratch_shapes=[pltpu.SemaphoreType.DMA((3,))],
            compiler_params=pltpu.CompilerParams(vmem_limit_bytes=4 * 2**20),
        )(*results)
        return jnp.swapaxes(commitment, 1, 2), dual, boundary

    return jax.shard_map(
        body,
        mesh=mesh,
        in_specs=(
            P(("groups", "area"), None, None),
            P(("groups", "area"), None, None),
            P(("groups", "area"), None, "scen"),
            P(("groups", "scen")),
            P(("groups", "area"), None, "scen"),
            P(("groups", "area"), None),
            P(("groups", "area")),
            P(("groups", "area"), None),
            P(("groups", "area")),
            P(("groups", "area")),
        ),
        out_specs=(
            P(("groups", "area"), None, None),
            P(("groups", "area"), None, "scen"),
            P(("groups", "area"), None, "scen"),
        ),
        check_vma=False,
    )
```

```python
import functools

import jax
import jax.numpy as jnp
from jax import lax
from jax.experimental import pallas as pl
from jax.experimental.pallas import tpu as pltpu
from jax.sharding import PartitionSpec as P

GEN = 128
BND = 32
MAXN = 4
LANES = 128
CHUNKS = 1
EARLY = 2
MESH = pl.DeviceIdType.MESH
F32 = jnp.float32
BF16 = jnp.bfloat16

penalty = 1.0


def dot(a, b):
    return jnp.dot(a, b, preferred_element_type=F32)


def halves(x, axis):
    high = x.astype(BF16)
    low = (x - high.astype(F32)).astype(BF16)
    return jnp.concatenate([high, low], axis=axis)


def kernel(
    n_area,
    n_scen,
    raw_hbm,
    near_hbm,
    live_hbm,
    gain_hbm,
    plants_hbm,
    inner_hbm,
    matrix_ref,
    mean_ref,
    spread_ref,
    prior_ref,
    commit_ref,
    dual_ref,
    bound_ref,
    raw_ref,
    near_ref,
    live_ref,
    gain_ref,
    plants_ref,
    inner_ref,
    rows_buf,
    mean_buf,
    spread_buf,
    prior_buf,
    couple_buf,
    base_buf,
    sums_buf,
    sums_in,
    small_buf,
    edge_in,
    direct_buf,
    total_buf,
    load_sem,
    word_sem,
    send_sem,
    recv_sem,
    scen_send,
    scen_recv,
    direct_send,
    direct_recv,
    turn_sem,
):
    order = matrix_ref.shape[2]
    columns = spread_ref.shape[2]
    hours = mean_ref.shape[1]
    scen_here = raw_ref.shape[0]
    rows = GEN + BND
    groups = LANES // hours
    width = columns // CHUNKS
    wide = n_area * BND
    me = lax.axis_index("area")
    scen = lax.axis_index("scen")

    others = [k + (k - me + n_area) // n_area for k in range(n_area - 1)]
    mine = pl.ds(pl.multiple_of(me * BND, BND), BND)
    rows_in = [
        pltpu.make_async_copy(
            matrix_ref.at[0, pl.ds(0, GEN)], rows_buf.at[pl.ds(0, GEN)], load_sem.at[0]
        ),
        pltpu.make_async_copy(
            matrix_ref.at[0, pl.ds(order - BND, BND)], rows_buf.at[pl.ds(GEN, BND)], load_sem.at[1]
        ),
    ]
    mean_in = pltpu.make_async_copy(mean_ref.at[0], mean_buf, load_sem.at[2])
    prior_in = pltpu.make_async_copy(prior_ref.at[0], prior_buf.at[mine], load_sem.at[3])
    parts = [pl.ds(c * width, width) for c in range(CHUNKS)]
    spread_in = [
        pltpu.make_async_copy(
            spread_ref.at[0, :, part], spread_buf.at[:, part], load_sem.at[4 + c]
        )
        for c, part in enumerate(parts)
    ]
    pairs = (
        (raw_hbm, raw_ref),
        (near_hbm, near_ref),
        (live_hbm, live_ref),
        (gain_hbm, gain_ref),
        (plants_hbm, plants_ref),
        (inner_hbm, inner_ref),
    )
    words = [
        pltpu.make_async_copy(source, target, word_sem.at[i])
        for i, (source, target) in enumerate(pairs)
    ]
    for load in [mean_in] + words + rows_in + [prior_in] + spread_in:
        load.start()
    barrier = pltpu.get_barrier_semaphore()
    lead = (me == 0) & (scen < EARLY)

    @pl.when(lead)
    def _():
        for area in others:
            for d in range(1, n_scen):
                peer = {"area": area, "scen": lax.rem(scen + d, n_scen)}
                pl.semaphore_signal(barrier, inc=1, device_id=peer, device_id_type=MESH)


    for d in range(1, n_area):
        pl.semaphore_signal(
            barrier, inc=1, device_id={"area": lax.rem(me + d, n_area)}, device_id_type=MESH
        )
    for d in range(1, n_scen):
        pl.semaphore_signal(
            barrier, inc=1, device_id={"scen": lax.rem(scen + d, n_scen)}, device_id_type=MESH
        )

    def to_area(ref, rows_of, kind, area):
        own = rows_of(me)
        return pltpu.make_async_remote_copy(
            src_ref=ref.at[own],
            dst_ref=ref.at[own],
            send_sem=send_sem.at[kind, area],
            recv_sem=recv_sem.at[kind, me],
            device_id={"area": area},
            device_id_type=MESH,
        )

    def arrived(ref, rows_of, kind):
        for area in others:
            theirs = ref.at[rows_of(area)]
            pltpu.make_async_remote_copy(
                src_ref=theirs,
                dst_ref=theirs,
                send_sem=send_sem.at[kind, area],
                recv_sem=recv_sem.at[kind, area],
                device_id={"area": area},
                device_id_type=MESH,
            ).wait_recv()

    def tie_rows(area):
        return pl.ds(pl.multiple_of(area * BND, BND), BND)

    def small_rows(area):
        return area

    kinds = ((prior_buf, tie_rows), (couple_buf, small_rows), (base_buf, tie_rows))
    bulk = [[to_area(*pair, i, a) for i, pair in enumerate(kinds)] for a in others]
    send_small = [to_area(small_buf, small_rows, 3, a) for a in others]

    def to_scens(ref, target, kind):
        return [
            pltpu.make_async_remote_copy(
                src_ref=ref,
                dst_ref=target.at[d - 1],
                send_sem=scen_send.at[kind, d - 1],
                recv_sem=scen_recv.at[kind, d - 1],
                device_id={"scen": lax.rem(scen + d, n_scen)},
                device_id_type=MESH,
            )
            for d in range(1, n_scen)
        ]

    send_sums = to_scens(sums_buf, sums_in, 0)
    send_edge = to_scens(small_buf, edge_in, 1)
    turns = [lax.rem(scen + d, n_scen) for d in range(n_scen)]

    def direct(target, area, source):
        return pltpu.make_async_remote_copy(
            src_ref=small_buf.at[me],
            dst_ref=direct_buf.at[area * n_scen + source],
            send_sem=direct_send.at[target],
            recv_sem=direct_recv.at[area * n_scen + source],
            device_id={"area": 0, "scen": target},
            device_id_type=MESH,
        )

    def send_direct(act):
        for target in range(EARLY):
            copy = direct(target, me, scen)

            @pl.when(scen != target)
            def _():
                act(copy)

    def send_edges(act):
        for d in range(1, n_scen):

            @pl.when((me > 0) | (turns[d] >= EARLY))
            def _():
                act(send_edge[d - 1])


    for word in words:
        word.wait()
    for load in rows_in:
        load.wait()
    pick_row = lax.broadcasted_iota(jnp.int32, (LANES, wide), 0)
    pick_col = lax.broadcasted_iota(jnp.int32, (LANES, wide), 1)
    pick = jnp.where(pick_row - (LANES - BND) == pick_col % BND, 1.0, 0.0).astype(BF16)
    area_of = lax.broadcasted_iota(jnp.int32, (1, wide), 1) // BND
    gain = jnp.zeros((1, wide), F32)
    for j in range(MAXN):
        factor = jnp.where(j < live_ref[0], gain_ref[0, j], 0.0)
        gain = gain + jnp.where(area_of == near_ref[0, j], factor, 0.0)
    corner = dot(rows_buf[:, order - LANES :], pick)
    couple = (corner * gain).astype(BF16)
    eights = BND // 8
    high = gain.astype(BF16).astype(F32)
    part_row = lax.broadcasted_iota(jnp.int32, (8, wide), 0)
    thin = jnp.zeros((8, wide), F32)
    for q in range(eights):
        thin = thin + jnp.where(area_of == q, corner[GEN + q * 8 : GEN + q * 8 + 8], 0.0)
    gains = jnp.where(part_row < 4, high, gain - high)
    couple_buf[me] = jnp.concatenate([thin, gains], axis=0).astype(BF16)

    place = lax.broadcasted_iota(jnp.int32, (1, order), 1)
    gone = (place >= GEN) & (place < order - BND) & (place - GEN >= inner_ref[0])
    keep = jnp.where(gone, 0.0, 1.0).astype(BF16)
    matrix = rows_buf[...] * keep
    lane = lax.broadcasted_iota(jnp.int32, (1, LANES), 1)
    hour_row = lax.broadcasted_iota(jnp.int32, (hours, LANES), 0)
    hour_col = lax.broadcasted_iota(jnp.int32, (hours, LANES), 1)
    same_hour = jnp.where(hour_row == hour_col % hours, 1.0, 0.0).astype(BF16)
    fold_row = lax.broadcasted_iota(jnp.int32, (LANES, LANES), 0)
    fold_col = lax.broadcasted_iota(jnp.int32, (LANES, LANES), 1)
    fold = jnp.where(fold_row % hours == fold_col % hours, 1.0, 0.0).astype(BF16)
    fold2 = jnp.concatenate([fold, fold], axis=0)
    mean_in.wait()
    level = lax.dot_general(
        matrix, mean_buf[...], (((1,), (1,)), ((), ())), preferred_element_type=F32
    )
    level = dot(halves(level, 1), jnp.concatenate([same_hour, same_hour], axis=0))
    scen_of = lax.broadcasted_iota(jnp.int32, (1, columns), 1) // hours
    weight = jnp.zeros((1, columns), F32)
    total = jnp.float32(0.0)
    for s in range(scen_here):
        weight = jnp.where(scen_of == s, raw_ref[s], weight)
        total = total + raw_ref[s]

    def squeeze(x):
        x = x * weight
        out = x[:, :LANES]
        for k in range(1, columns // LANES):
            out = out + x[:, k * LANES : (k + 1) * LANES]
        return out

    def pack(x):
        step = x.shape[0] // groups
        out = x[:step] * spot[0]
        for k in range(1, groups):
            out = out + x[k * step : (k + 1) * step] * spot[k]
        return out

    prior_in.wait()
    old = squeeze(prior_buf[mine, :].astype(F32))
    states = []
    for load, part in zip(spread_in, parts):
        load.wait()
        states.append(
            dot(matrix, spread_buf[:, part]) + jnp.concatenate([level] * (width // LANES), axis=1)
        )
    state = jnp.concatenate(states, axis=1)

    far = (me + n_area - 1) // n_area
    late = (scen + n_scen - EARLY) // n_scen
    pl.semaphore_wait(barrier, n_area + n_scen - 2 + far * (EARLY - 1 + late))
    for some in bulk:
        some[1].start()
    spot = [jnp.where(lane // hours == k, 1.0, 0.0) for k in range(groups)]
    folded = jnp.concatenate([squeeze(state[GEN:]), old], axis=0)
    small_buf[me] = pack(dot(halves(folded, 1), fold2)).astype(BF16)

    send_direct(lambda copy: copy.start())
    for copy in send_small:
        copy.start()

    base_buf[mine, :] = state[GEN:].astype(BF16)

    gen_rows = GEN // groups
    folded = dot(halves(squeeze(state[:GEN]), 1), fold2)
    sums = jnp.concatenate([pack(folded), jnp.full((8, LANES), total, F32)], axis=0)
    sums_buf[...] = sums
    for copy in send_sums:
        copy.start()
    odd = (me > 0) & (scen == 1)
    even = (me > 0) & (scen == 0)
    held = (me == n_area - 1) & (scen < EARLY)
    bulk[0][0].start()

    @pl.when(jnp.logical_not(odd))
    def _():
        bulk[0][2].start()

    for k in range(1, n_area - 1):

        @pl.when(k >= me)
        def _():
            for copy in bulk[k][::2]:
                copy.start()

    for k in range(1, n_area - 1):

        @pl.when((k < me) & jnp.logical_not(held))
        def _():
            bulk[k][0].start()

    @pl.when(odd)
    def _():
        pl.semaphore_wait(turn_sem, 1)
        bulk[0][2].start()

    for copy in bulk[0][:2]:
        copy.wait_send()

    @pl.when(even)
    def _():
        pl.semaphore_signal(
            turn_sem, inc=1, device_id={"scen": scen + 1}, device_id_type=MESH
        )

    for k in range(1, n_area - 1):

        @pl.when((k < me) & held)
        def _():
            bulk[k][0].start()

        @pl.when(k < me)
        def _():
            bulk[k][2].start()

    arrived(small_buf, small_rows, 3)
    send_edges(lambda copy: copy.start())

    arrived(prior_buf, tie_rows, 0)
    arrived(couple_buf, small_rows, 1)
    prior = prior_buf[...]
    thin = couple_buf[...].astype(F32)
    slots = [jnp.where(lane // BND == q, 1.0, 0.0) for q in range(eights)]
    couples = jnp.concatenate(
        [thin[b, :8, :LANES] * slots[q] for b in range(n_area) for q in range(eights)], axis=0
    )
    tie_row = lax.broadcasted_iota(jnp.int32, (LANES, wide), 0)
    same_tie = jnp.where(tie_row % BND == pick_col % BND, 1.0, 0.0).astype(BF16)
    gains = jnp.concatenate(
        [jnp.broadcast_to(thin[b, 8:9] + thin[b, 12:13], (BND, wide)) for b in range(n_area)],
        axis=0,
    )
    couples = (dot(couples.astype(BF16), same_tie) * gains).astype(BF16)
    first = state[:GEN] + dot(couple[:GEN], prior)
    edge = dot(couples, prior).astype(BF16)
    gen_part = matrix[:, :GEN]
    later = state - penalty * dot(gen_part, first.astype(BF16)) + dot(couple, edge)

    for copy in send_sums:
        copy.wait_recv()
    for d in range(1, n_scen):
        sums = sums + sums_in[d - 1]
    scale = 1.0 / sums[gen_rows:]
    means = sums[:gen_rows] * jnp.concatenate([scale] * (gen_rows // 8), axis=0)
    gen_mean = jnp.concatenate([means[:gen_rows] * spot[k] for k in range(groups)], axis=0)
    gen_mean = dot(halves(gen_mean, 1), fold2)
    total_buf[...] = small_buf[...].astype(F32).reshape(total_buf.shape)

    @pl.when(lead)
    def _():
        for area in range(n_area):
            rows_of = slice(area * 8, (area + 1) * 8)
            for d in range(1, n_scen):
                direct(0, area, turns[d]).wait_recv()
                total_buf[rows_of] += direct_buf[area * n_scen + turns[d]].astype(F32)

    @pl.when(jnp.logical_not(lead))
    def _():
        for copy in send_edge:
            copy.wait_recv()
        for d in range(1, n_scen):
            total_buf[...] += edge_in[d - 1].astype(F32).reshape(total_buf.shape)

    small = total_buf[...]
    small = small * jnp.concatenate([scale] * n_area, axis=0)
    half = groups // 2
    edges = jnp.concatenate(
        [
            small[b * 8 : (b + 1) * 8] * spot[k + first_k]
            for first_k in (0, half)
            for b in range(n_area)
            for k in range(half)
        ],
        axis=0,
    )
    edges = dot(halves(edges, 1), fold2)
    prior_mean = edges[wide:].astype(BF16)
    edge_mean = (edges[:wide] + dot(couples, prior_mean)).astype(BF16)
    mean1 = gen_mean + dot(couple[:GEN], prior_mean)
    slot = lax.broadcasted_iota(jnp.int32, (GEN, LANES), 0)
    alive = jnp.where(slot < plants_ref[0], 1.0, 0.0)
    commit1 = jnp.clip(mean1, 0.0, 1.0) * alive
    both = jnp.concatenate([gen_part, gen_part], axis=1)
    mean2 = (
        gen_mean
        + penalty * dot(both[:GEN], halves(2.0 * commit1 - mean1, 0))
        + dot(couple[:GEN], edge_mean)
    )
    commit2 = jnp.clip(mean2, 0.0, 1.0) * alive
    push = dot(both, halves((2.0 * penalty) * commit1, 0))
    times = columns // LANES
    drop = jnp.concatenate([push[:GEN] - commit1 - commit2] * times, axis=1) + first
    commit_ref[0] = commit2.T[:hours]

    arrived(base_buf, tie_rows, 2)
    state2 = later + dot(couple, base_buf[...])
    dual_ref[0] = state2[:GEN] + drop
    bound_ref[0] = state2[GEN:] + jnp.concatenate([push[GEN:]] * times, axis=1)

    for copy in sum(bulk[1:], send_small + send_sums + bulk[0][2:]):
        copy.wait_send()
    send_direct(lambda copy: copy.wait_send())
    send_edges(lambda copy: copy.wait_send())


def place(*refs):
    count = (len(refs) - 1) // 2
    sems = refs[-1]
    copies = [
        pltpu.make_async_copy(refs[i], refs[count + i], sems.at[i]) for i in range(count)
    ]
    for copy in copies:
        copy.start()
    for copy in copies:
        copy.wait()


def solution(mesh):
    n_area, n_scen = mesh.shape["area"], mesh.shape["scen"]

    def body(matrix, mean, spread, raw, prior, near, live, gain, plants, inner):
        order, columns, hours = matrix.shape[2], spread.shape[2], mean.shape[2]
        hbm = pl.BlockSpec(memory_space=pltpu.HBM)
        vmem = pl.BlockSpec(memory_space=pltpu.VMEM)
        rows = GEN + BND
        wide = n_area * BND
        packed = GEN * hours // LANES + 8
        results = pl.pallas_call(
            functools.partial(kernel, n_area, n_scen),
            out_shape=(
                pltpu.VMEM((1, hours, GEN), F32),
                pltpu.VMEM((1, GEN, columns), F32),
                pltpu.VMEM((1, BND, columns), F32),
            ),
            in_specs=[hbm] * 10,
            out_specs=(vmem,) * 3,
            scratch_shapes=[
                pltpu.SMEM(raw.shape, raw.dtype),
                pltpu.SMEM(near.shape, near.dtype),
                pltpu.SMEM(live.shape, live.dtype),
                pltpu.SMEM(gain.shape, gain.dtype),
                pltpu.SMEM(plants.shape, plants.dtype),
                pltpu.SMEM(inner.shape, inner.dtype),
                pltpu.VMEM((rows, order), BF16),
                pltpu.VMEM((hours, order), BF16),
                pltpu.VMEM((order, columns), BF16),
                pltpu.VMEM((wide, columns), BF16),
                pltpu.VMEM((n_area, 16, wide), BF16),
                pltpu.VMEM((wide, columns), BF16),
                pltpu.VMEM((packed, LANES), F32),
                pltpu.VMEM((n_scen - 1, packed, LANES), F32),
                pltpu.VMEM((n_area, 8, LANES), BF16),
                pltpu.VMEM((n_scen - 1, n_area, 8, LANES), BF16),
                pltpu.VMEM((n_area * n_scen, 8, LANES), BF16),
                pltpu.VMEM((n_area * 8, LANES), F32),
                pltpu.SemaphoreType.DMA((4 + CHUNKS,)),
                pltpu.SemaphoreType.DMA((6,)),
                pltpu.SemaphoreType.DMA((4, n_area)),
                pltpu.SemaphoreType.DMA((4, n_area)),
                pltpu.SemaphoreType.DMA((2, n_scen - 1)),
                pltpu.SemaphoreType.DMA((2, n_scen - 1)),
                pltpu.SemaphoreType.DMA((EARLY,)),
                pltpu.SemaphoreType.DMA((n_area * n_scen,)),
                pltpu.SemaphoreType.REGULAR,
            ],
            compiler_params=pltpu.CompilerParams(
                collective_id=0, has_side_effects=True, vmem_limit_bytes=67043328 - 360 * 2**10
            ),
        )(
            raw,
            near,
            live,
            gain,
            plants,
            inner,
            matrix,
            jnp.swapaxes(mean, 1, 2),
            spread,
            prior,
        )
        commitment, dual, boundary = pl.pallas_call(
            place,
            out_shape=tuple(jax.ShapeDtypeStruct(x.shape, x.dtype) for x in results),
            in_specs=(vmem,) * 3,
            out_specs=(hbm,) * 3,
            scratch_shapes=[pltpu.SemaphoreType.DMA((3,))],
            compiler_params=pltpu.CompilerParams(vmem_limit_bytes=4 * 2**20),
        )(*results)
        return jnp.swapaxes(commitment, 1, 2), dual, boundary

    return jax.shard_map(
        body,
        mesh=mesh,
        in_specs=(
            P(("groups", "area"), None, None),
            P(("groups", "area"), None, None),
            P(("groups", "area"), None, "scen"),
            P(("groups", "scen")),
            P(("groups", "area"), None, "scen"),
            P(("groups", "area"), None),
            P(("groups", "area")),
            P(("groups", "area"), None),
            P(("groups", "area")),
            P(("groups", "area")),
        ),
        out_specs=(
            P(("groups", "area"), None, None),
            P(("groups", "area"), None, "scen"),
            P(("groups", "area"), None, "scen"),
        ),
        check_vma=False,
    )
```

```python
import functools

import jax
import jax.numpy as jnp
from jax import lax
from jax.experimental import pallas as pl
from jax.experimental.pallas import tpu as pltpu
from jax.sharding import PartitionSpec as P

GEN = 128
BND = 32
MAXN = 4
LANES = 128
CHUNKS = 1
EARLY = 2
MESH = pl.DeviceIdType.MESH
F32 = jnp.float32
BF16 = jnp.bfloat16

penalty = 1.0


def dot(a, b):
    return jnp.dot(a, b, preferred_element_type=F32)


def halves(x, axis):
    high = x.astype(BF16)
    low = (x - high.astype(F32)).astype(BF16)
    return jnp.concatenate([high, low], axis=axis)


def kernel(
    n_area,
    n_scen,
    raw_hbm,
    near_hbm,
    live_hbm,
    gain_hbm,
    plants_hbm,
    inner_hbm,
    matrix_ref,
    mean_ref,
    spread_ref,
    prior_ref,
    commit_ref,
    dual_ref,
    bound_ref,
    raw_ref,
    near_ref,
    live_ref,
    gain_ref,
    plants_ref,
    inner_ref,
    rows_buf,
    mean_buf,
    spread_buf,
    prior_buf,
    couple_buf,
    base_buf,
    sums_buf,
    sums_in,
    small_buf,
    edge_in,
    direct_buf,
    total_buf,
    load_sem,
    word_sem,
    send_sem,
    recv_sem,
    scen_send,
    scen_recv,
    direct_send,
    direct_recv,
    turn_sem,
):
    order = matrix_ref.shape[2]
    columns = spread_ref.shape[2]
    hours = mean_ref.shape[1]
    scen_here = raw_ref.shape[0]
    rows = GEN + BND
    groups = LANES // hours
    width = columns // CHUNKS
    wide = n_area * BND
    me = lax.axis_index("area")
    scen = lax.axis_index("scen")

    others = [k + (k - me + n_area) // n_area for k in range(n_area - 1)]
    mine = pl.ds(pl.multiple_of(me * BND, BND), BND)
    rows_in = [
        pltpu.make_async_copy(
            matrix_ref.at[0, pl.ds(0, GEN)], rows_buf.at[pl.ds(0, GEN)], load_sem.at[0]
        ),
        pltpu.make_async_copy(
            matrix_ref.at[0, pl.ds(order - BND, BND)], rows_buf.at[pl.ds(GEN, BND)], load_sem.at[1]
        ),
    ]
    mean_in = pltpu.make_async_copy(mean_ref.at[0], mean_buf, load_sem.at[2])
    prior_in = pltpu.make_async_copy(prior_ref.at[0], prior_buf.at[mine], load_sem.at[3])
    parts = [pl.ds(c * width, width) for c in range(CHUNKS)]
    spread_in = [
        pltpu.make_async_copy(
            spread_ref.at[0, :, part], spread_buf.at[:, part], load_sem.at[4 + c]
        )
        for c, part in enumerate(parts)
    ]
    pairs = (
        (raw_hbm, raw_ref),
        (near_hbm, near_ref),
        (live_hbm, live_ref),
        (gain_hbm, gain_ref),
        (plants_hbm, plants_ref),
        (inner_hbm, inner_ref),
    )
    words = [
        pltpu.make_async_copy(source, target, word_sem.at[i])
        for i, (source, target) in enumerate(pairs)
    ]
    for load in [mean_in] + words + rows_in + [prior_in] + spread_in:
        load.start()
    barrier = pltpu.get_barrier_semaphore()
    lead = (me == 0) & (scen < EARLY)

    @pl.when(lead)
    def _():
        for area in others:
            for d in range(1, n_scen):
                peer = {"area": area, "scen": lax.rem(scen + d, n_scen)}
                pl.semaphore_signal(barrier, inc=1, device_id=peer, device_id_type=MESH)


    for d in range(1, n_area):
        pl.semaphore_signal(
            barrier, inc=1, device_id={"area": lax.rem(me + d, n_area)}, device_id_type=MESH
        )
    for d in range(1, n_scen):
        pl.semaphore_signal(
            barrier, inc=1, device_id={"scen": lax.rem(scen + d, n_scen)}, device_id_type=MESH
        )

    def to_area(ref, rows_of, kind, area):
        own = rows_of(me)
        return pltpu.make_async_remote_copy(
            src_ref=ref.at[own],
            dst_ref=ref.at[own],
            send_sem=send_sem.at[kind, area],
            recv_sem=recv_sem.at[kind, me],
            device_id={"area": area},
            device_id_type=MESH,
        )

    def arrived(ref, rows_of, kind):
        for area in others:
            theirs = ref.at[rows_of(area)]
            pltpu.make_async_remote_copy(
                src_ref=theirs,
                dst_ref=theirs,
                send_sem=send_sem.at[kind, area],
                recv_sem=recv_sem.at[kind, area],
                device_id={"area": area},
                device_id_type=MESH,
            ).wait_recv()

    def tie_rows(area):
        return pl.ds(pl.multiple_of(area * BND, BND), BND)

    def small_rows(area):
        return area

    kinds = ((prior_buf, tie_rows), (couple_buf, small_rows), (base_buf, tie_rows))
    bulk = [[to_area(*pair, i, a) for i, pair in enumerate(kinds)] for a in others]
    send_small = [to_area(small_buf, small_rows, 3, a) for a in others]

    def to_scens(ref, target, kind):
        return [
            pltpu.make_async_remote_copy(
                src_ref=ref,
                dst_ref=target.at[d - 1],
                send_sem=scen_send.at[kind, d - 1],
                recv_sem=scen_recv.at[kind, d - 1],
                device_id={"scen": lax.rem(scen + d, n_scen)},
                device_id_type=MESH,
            )
            for d in range(1, n_scen)
        ]

    send_sums = to_scens(sums_buf, sums_in, 0)
    send_edge = to_scens(small_buf, edge_in, 1)
    turns = [lax.rem(scen + d, n_scen) for d in range(n_scen)]

    def direct(target, area, source):
        return pltpu.make_async_remote_copy(
            src_ref=small_buf.at[me],
            dst_ref=direct_buf.at[area * n_scen + source],
            send_sem=direct_send.at[target],
            recv_sem=direct_recv.at[area * n_scen + source],
            device_id={"area": 0, "scen": target},
            device_id_type=MESH,
        )

    def send_direct(act):
        for target in range(EARLY):
            copy = direct(target, me, scen)

            @pl.when(scen != target)
            def _():
                act(copy)

    def send_edges(act):
        for d in range(1, n_scen):

            @pl.when((me > 0) | (turns[d] >= EARLY))
            def _():
                act(send_edge[d - 1])


    for word in words:
        word.wait()
    for load in rows_in:
        load.wait()
    pick_row = lax.broadcasted_iota(jnp.int32, (LANES, wide), 0)
    pick_col = lax.broadcasted_iota(jnp.int32, (LANES, wide), 1)
    pick = jnp.where(pick_row - (LANES - BND) == pick_col % BND, 1.0, 0.0).astype(BF16)
    area_of = lax.broadcasted_iota(jnp.int32, (1, wide), 1) // BND
    gain = jnp.zeros((1, wide), F32)
    for j in range(MAXN):
        factor = jnp.where(j < live_ref[0], gain_ref[0, j], 0.0)
        gain = gain + jnp.where(area_of == near_ref[0, j], factor, 0.0)
    corner = dot(rows_buf[:, order - LANES :], pick)
    couple = (corner * gain).astype(BF16)
    eights = BND // 8
    high = gain.astype(BF16).astype(F32)
    part_row = lax.broadcasted_iota(jnp.int32, (8, wide), 0)
    thin = jnp.zeros((8, wide), F32)
    for q in range(eights):
        thin = thin + jnp.where(area_of == q, corner[GEN + q * 8 : GEN + q * 8 + 8], 0.0)
    gains = jnp.where(part_row < 4, high, gain - high)
    couple_buf[me] = jnp.concatenate([thin, gains], axis=0).astype(BF16)

    place = lax.broadcasted_iota(jnp.int32, (1, order), 1)
    gone = (place >= GEN) & (place < order - BND) & (place - GEN >= inner_ref[0])
    keep = jnp.where(gone, 0.0, 1.0).astype(BF16)
    matrix = rows_buf[...] * keep
    lane = lax.broadcasted_iota(jnp.int32, (1, LANES), 1)
    hour_row = lax.broadcasted_iota(jnp.int32, (hours, LANES), 0)
    hour_col = lax.broadcasted_iota(jnp.int32, (hours, LANES), 1)
    same_hour = jnp.where(hour_row == hour_col % hours, 1.0, 0.0).astype(BF16)
    fold_row = lax.broadcasted_iota(jnp.int32, (LANES, LANES), 0)
    fold_col = lax.broadcasted_iota(jnp.int32, (LANES, LANES), 1)
    fold = jnp.where(fold_row % hours == fold_col % hours, 1.0, 0.0).astype(BF16)
    fold2 = jnp.concatenate([fold, fold], axis=0)
    mean_in.wait()
    level = lax.dot_general(
        matrix, mean_buf[...], (((1,), (1,)), ((), ())), preferred_element_type=F32
    )
    level = dot(halves(level, 1), jnp.concatenate([same_hour, same_hour], axis=0))
    scen_of = lax.broadcasted_iota(jnp.int32, (1, columns), 1) // hours
    weight = jnp.zeros((1, columns), F32)
    total = jnp.float32(0.0)
    for s in range(scen_here):
        weight = jnp.where(scen_of == s, raw_ref[s], weight)
        total = total + raw_ref[s]

    def squeeze(x):
        x = x * weight
        out = x[:, :LANES]
        for k in range(1, columns // LANES):
            out = out + x[:, k * LANES : (k + 1) * LANES]
        return out

    def pack(x):
        step = x.shape[0] // groups
        out = x[:step] * spot[0]
        for k in range(1, groups):
            out = out + x[k * step : (k + 1) * step] * spot[k]
        return out

    prior_in.wait()
    old = squeeze(prior_buf[mine, :].astype(F32))
    states = []
    for load, part in zip(spread_in, parts):
        load.wait()
        states.append(
            dot(matrix, spread_buf[:, part]) + jnp.concatenate([level] * (width // LANES), axis=1)
        )
    state = jnp.concatenate(states, axis=1)

    far = (me + n_area - 1) // n_area
    late = (scen + n_scen - EARLY) // n_scen
    pl.semaphore_wait(barrier, n_area + n_scen - 2 + far * (EARLY - 1 + late))
    for some in bulk:
        some[1].start()
    spot = [jnp.where(lane // hours == k, 1.0, 0.0) for k in range(groups)]
    folded = jnp.concatenate([squeeze(state[GEN:]), old], axis=0)
    small_buf[me] = pack(dot(folded.astype(BF16), fold)).astype(BF16)

    send_direct(lambda copy: copy.start())
    for copy in send_small:
        copy.start()

    base_buf[mine, :] = state[GEN:].astype(BF16)

    gen_rows = GEN // groups
    folded = dot(halves(squeeze(state[:GEN]), 1), fold2)
    sums = jnp.concatenate([pack(folded), jnp.full((8, LANES), total, F32)], axis=0)
    sums_buf[...] = sums
    for copy in send_sums:
        copy.start()
    odd = (me > 0) & (scen == 1)
    even = (me > 0) & (scen == 0)
    held = (me == n_area - 1) & (scen < EARLY)
    bulk[0][0].start()

    @pl.when(jnp.logical_not(odd))
    def _():
        bulk[0][2].start()

    for k in range(1, n_area - 1):

        @pl.when(k >= me)
        def _():
            for copy in bulk[k][::2]:
                copy.start()

    for k in range(1, n_area - 1):

        @pl.when((k < me) & jnp.logical_not(held))
        def _():
            bulk[k][0].start()

    @pl.when(odd)
    def _():
        pl.semaphore_wait(turn_sem, 1)
        bulk[0][2].start()

    for copy in bulk[0][:2]:
        copy.wait_send()

    @pl.when(even)
    def _():
        pl.semaphore_signal(
            turn_sem, inc=1, device_id={"scen": scen + 1}, device_id_type=MESH
        )

    for k in range(1, n_area - 1):

        @pl.when((k < me) & held)
        def _():
            bulk[k][0].start()

        @pl.when(k < me)
        def _():
            bulk[k][2].start()

    arrived(small_buf, small_rows, 3)
    send_edges(lambda copy: copy.start())

    arrived(prior_buf, tie_rows, 0)
    arrived(couple_buf, small_rows, 1)
    prior = prior_buf[...]
    thin = couple_buf[...].astype(F32)
    slots = [jnp.where(lane // BND == q, 1.0, 0.0) for q in range(eights)]
    couples = jnp.concatenate(
        [thin[b, :8, :LANES] * slots[q] for b in range(n_area) for q in range(eights)], axis=0
    )
    tie_row = lax.broadcasted_iota(jnp.int32, (LANES, wide), 0)
    same_tie = jnp.where(tie_row % BND == pick_col % BND, 1.0, 0.0).astype(BF16)
    gains = jnp.concatenate(
        [jnp.broadcast_to(thin[b, 8:9] + thin[b, 12:13], (BND, wide)) for b in range(n_area)],
        axis=0,
    )
    couples = (dot(couples.astype(BF16), same_tie) * gains).astype(BF16)
    first = state[:GEN] + dot(couple[:GEN], prior)
    edge = dot(couples, prior).astype(BF16)
    gen_part = matrix[:, :GEN]
    later = state - penalty * dot(gen_part, first.astype(BF16)) + dot(couple, edge)

    for copy in send_sums:
        copy.wait_recv()
    for d in range(1, n_scen):
        sums = sums + sums_in[d - 1]
    scale = 1.0 / sums[gen_rows:]
    means = sums[:gen_rows] * jnp.concatenate([scale] * (gen_rows // 8), axis=0)
    gen_mean = jnp.concatenate([means[:gen_rows] * spot[k] for k in range(groups)], axis=0)
    gen_mean = dot(halves(gen_mean, 1), fold2)
    total_buf[...] = small_buf[...].astype(F32).reshape(total_buf.shape)

    @pl.when(lead)
    def _():
        for area in range(n_area):
            rows_of = slice(area * 8, (area + 1) * 8)
            for d in range(1, n_scen):
                direct(0, area, turns[d]).wait_recv()
                total_buf[rows_of] += direct_buf[area * n_scen + turns[d]].astype(F32)

    @pl.when(jnp.logical_not(lead))
    def _():
        for copy in send_edge:
            copy.wait_recv()
        for d in range(1, n_scen):
            total_buf[...] += edge_in[d - 1].astype(F32).reshape(total_buf.shape)

    small = total_buf[...]
    small = small * jnp.concatenate([scale] * n_area, axis=0)
    half = groups // 2
    edges = jnp.concatenate(
        [
            small[b * 8 : (b + 1) * 8] * spot[k + first_k]
            for first_k in (0, half)
            for b in range(n_area)
            for k in range(half)
        ],
        axis=0,
    )
    edges = dot(edges.astype(BF16), fold)
    prior_mean = edges[wide:].astype(BF16)
    edge_mean = (edges[:wide] + dot(couples, prior_mean)).astype(BF16)
    mean1 = gen_mean + dot(couple[:GEN], prior_mean)
    slot = lax.broadcasted_iota(jnp.int32, (GEN, LANES), 0)
    alive = jnp.where(slot < plants_ref[0], 1.0, 0.0)
    commit1 = jnp.clip(mean1, 0.0, 1.0) * alive
    both = jnp.concatenate([gen_part, gen_part], axis=1)
    mean2 = (
        gen_mean
        + penalty * dot(both[:GEN], halves(2.0 * commit1 - mean1, 0))
        + dot(couple[:GEN], edge_mean)
    )
    commit2 = jnp.clip(mean2, 0.0, 1.0) * alive
    push = dot(both, halves((2.0 * penalty) * commit1, 0))
    times = columns // LANES
    drop = jnp.concatenate([push[:GEN] - commit1 - commit2] * times, axis=1) + first
    commit_ref[0] = commit2.T[:hours]

    arrived(base_buf, tie_rows, 2)
    state2 = later + dot(couple, base_buf[...])
    dual_ref[0] = state2[:GEN] + drop
    bound_ref[0] = state2[GEN:] + jnp.concatenate([push[GEN:]] * times, axis=1)

    for copy in sum(bulk[1:], send_small + send_sums + bulk[0][2:]):
        copy.wait_send()
    send_direct(lambda copy: copy.wait_send())
    send_edges(lambda copy: copy.wait_send())


def place(*refs):
    count = (len(refs) - 1) // 2
    sems = refs[-1]
    copies = [
        pltpu.make_async_copy(refs[i], refs[count + i], sems.at[i]) for i in range(count)
    ]
    for copy in copies:
        copy.start()
    for copy in copies:
        copy.wait()


def solution(mesh):
    n_area, n_scen = mesh.shape["area"], mesh.shape["scen"]

    def body(matrix, mean, spread, raw, prior, near, live, gain, plants, inner):
        order, columns, hours = matrix.shape[2], spread.shape[2], mean.shape[2]
        hbm = pl.BlockSpec(memory_space=pltpu.HBM)
        vmem = pl.BlockSpec(memory_space=pltpu.VMEM)
        rows = GEN + BND
        wide = n_area * BND
        packed = GEN * hours // LANES + 8
        results = pl.pallas_call(
            functools.partial(kernel, n_area, n_scen),
            out_shape=(
                pltpu.VMEM((1, hours, GEN), F32),
                pltpu.VMEM((1, GEN, columns), F32),
                pltpu.VMEM((1, BND, columns), F32),
            ),
            in_specs=[hbm] * 10,
            out_specs=(vmem,) * 3,
            scratch_shapes=[
                pltpu.SMEM(raw.shape, raw.dtype),
                pltpu.SMEM(near.shape, near.dtype),
                pltpu.SMEM(live.shape, live.dtype),
                pltpu.SMEM(gain.shape, gain.dtype),
                pltpu.SMEM(plants.shape, plants.dtype),
                pltpu.SMEM(inner.shape, inner.dtype),
                pltpu.VMEM((rows, order), BF16),
                pltpu.VMEM((hours, order), BF16),
                pltpu.VMEM((order, columns), BF16),
                pltpu.VMEM((wide, columns), BF16),
                pltpu.VMEM((n_area, 16, wide), BF16),
                pltpu.VMEM((wide, columns), BF16),
                pltpu.VMEM((packed, LANES), F32),
                pltpu.VMEM((n_scen - 1, packed, LANES), F32),
                pltpu.VMEM((n_area, 8, LANES), BF16),
                pltpu.VMEM((n_scen - 1, n_area, 8, LANES), BF16),
                pltpu.VMEM((n_area * n_scen, 8, LANES), BF16),
                pltpu.VMEM((n_area * 8, LANES), F32),
                pltpu.SemaphoreType.DMA((4 + CHUNKS,)),
                pltpu.SemaphoreType.DMA((6,)),
                pltpu.SemaphoreType.DMA((4, n_area)),
                pltpu.SemaphoreType.DMA((4, n_area)),
                pltpu.SemaphoreType.DMA((2, n_scen - 1)),
                pltpu.SemaphoreType.DMA((2, n_scen - 1)),
                pltpu.SemaphoreType.DMA((EARLY,)),
                pltpu.SemaphoreType.DMA((n_area * n_scen,)),
                pltpu.SemaphoreType.REGULAR,
            ],
            compiler_params=pltpu.CompilerParams(
                collective_id=0, has_side_effects=True, vmem_limit_bytes=67043328 - 360 * 2**10
            ),
        )(
            raw,
            near,
            live,
            gain,
            plants,
            inner,
            matrix,
            jnp.swapaxes(mean, 1, 2),
            spread,
            prior,
        )
        commitment, dual, boundary = pl.pallas_call(
            place,
            out_shape=tuple(jax.ShapeDtypeStruct(x.shape, x.dtype) for x in results),
            in_specs=(vmem,) * 3,
            out_specs=(hbm,) * 3,
            scratch_shapes=[pltpu.SemaphoreType.DMA((3,))],
            compiler_params=pltpu.CompilerParams(vmem_limit_bytes=4 * 2**20),
        )(*results)
        return jnp.swapaxes(commitment, 1, 2), dual, boundary

    return jax.shard_map(
        body,
        mesh=mesh,
        in_specs=(
            P(("groups", "area"), None, None),
            P(("groups", "area"), None, None),
            P(("groups", "area"), None, "scen"),
            P(("groups", "scen")),
            P(("groups", "area"), None, "scen"),
            P(("groups", "area"), None),
            P(("groups", "area")),
            P(("groups", "area"), None),
            P(("groups", "area")),
            P(("groups", "area")),
        ),
        out_specs=(
            P(("groups", "area"), None, None),
            P(("groups", "area"), None, "scen"),
            P(("groups", "area"), None, "scen"),
        ),
        check_vma=False,
    )
```

```python
import functools

import jax
import jax.numpy as jnp
from jax import lax
from jax.experimental import pallas as pl
from jax.experimental.pallas import tpu as pltpu
from jax.sharding import PartitionSpec as P

GEN = 128
BND = 32
MAXN = 4
LANES = 128
CHUNKS = 1
EARLY = 2
MESH = pl.DeviceIdType.MESH
F32 = jnp.float32
BF16 = jnp.bfloat16

penalty = 1.0


def dot(a, b):
    return jnp.dot(a, b, preferred_element_type=F32)


def halves(x, axis):
    high = x.astype(BF16)
    low = (x - high.astype(F32)).astype(BF16)
    return jnp.concatenate([high, low], axis=axis)


def kernel(
    n_area,
    n_scen,
    raw_hbm,
    near_hbm,
    live_hbm,
    gain_hbm,
    plants_hbm,
    inner_hbm,
    matrix_ref,
    mean_ref,
    spread_ref,
    prior_ref,
    commit_ref,
    dual_ref,
    bound_ref,
    raw_ref,
    near_ref,
    live_ref,
    gain_ref,
    plants_ref,
    inner_ref,
    rows_buf,
    mean_buf,
    spread_buf,
    prior_buf,
    couple_buf,
    base_buf,
    sums_buf,
    sums_in,
    small_buf,
    edge_in,
    direct_buf,
    total_buf,
    load_sem,
    word_sem,
    send_sem,
    recv_sem,
    scen_send,
    scen_recv,
    direct_send,
    direct_recv,
    turn_sem,
):
    order = matrix_ref.shape[2]
    columns = spread_ref.shape[2]
    hours = mean_ref.shape[1]
    scen_here = raw_ref.shape[0]
    rows = GEN + BND
    groups = LANES // hours
    width = columns // CHUNKS
    wide = n_area * BND
    me = lax.axis_index("area")
    scen = lax.axis_index("scen")

    others = [k + (k - me + n_area) // n_area for k in range(n_area - 1)]
    mine = pl.ds(pl.multiple_of(me * BND, BND), BND)
    rows_in = [
        pltpu.make_async_copy(
            matrix_ref.at[0, pl.ds(0, GEN)], rows_buf.at[pl.ds(0, GEN)], load_sem.at[0]
        ),
        pltpu.make_async_copy(
            matrix_ref.at[0, pl.ds(order - BND, BND)], rows_buf.at[pl.ds(GEN, BND)], load_sem.at[1]
        ),
    ]
    mean_in = pltpu.make_async_copy(mean_ref.at[0], mean_buf, load_sem.at[2])
    prior_in = pltpu.make_async_copy(prior_ref.at[0], prior_buf.at[mine], load_sem.at[3])
    parts = [pl.ds(c * width, width) for c in range(CHUNKS)]
    spread_in = [
        pltpu.make_async_copy(
            spread_ref.at[0, :, part], spread_buf.at[:, part], load_sem.at[4 + c]
        )
        for c, part in enumerate(parts)
    ]
    pairs = (
        (raw_hbm, raw_ref),
        (near_hbm, near_ref),
        (live_hbm, live_ref),
        (gain_hbm, gain_ref),
        (plants_hbm, plants_ref),
        (inner_hbm, inner_ref),
    )
    words = [
        pltpu.make_async_copy(source, target, word_sem.at[i])
        for i, (source, target) in enumerate(pairs)
    ]
    for load in [mean_in] + words + rows_in + [prior_in] + spread_in:
        load.start()
    barrier = pltpu.get_barrier_semaphore()
    lead = (me == 0) & (scen < EARLY)

    @pl.when(lead)
    def _():
        for area in others:
            for d in range(1, n_scen):
                peer = {"area": area, "scen": lax.rem(scen + d, n_scen)}
                pl.semaphore_signal(barrier, inc=1, device_id=peer, device_id_type=MESH)


    for d in range(1, n_area):
        pl.semaphore_signal(
            barrier, inc=1, device_id={"area": lax.rem(me + d, n_area)}, device_id_type=MESH
        )
    for d in range(1, n_scen):
        pl.semaphore_signal(
            barrier, inc=1, device_id={"scen": lax.rem(scen + d, n_scen)}, device_id_type=MESH
        )

    def to_area(ref, rows_of, kind, area):
        own = rows_of(me)
        return pltpu.make_async_remote_copy(
            src_ref=ref.at[own],
            dst_ref=ref.at[own],
            send_sem=send_sem.at[kind, area],
            recv_sem=recv_sem.at[kind, me],
            device_id={"area": area},
            device_id_type=MESH,
        )

    def arrived(ref, rows_of, kind):
        for area in others:
            theirs = ref.at[rows_of(area)]
            pltpu.make_async_remote_copy(
                src_ref=theirs,
                dst_ref=theirs,
                send_sem=send_sem.at[kind, area],
                recv_sem=recv_sem.at[kind, area],
                device_id={"area": area},
                device_id_type=MESH,
            ).wait_recv()

    def tie_rows(area):
        return pl.ds(pl.multiple_of(area * BND, BND), BND)

    def small_rows(area):
        return area

    kinds = ((prior_buf, tie_rows), (couple_buf, small_rows), (base_buf, tie_rows))
    bulk = [[to_area(*pair, i, a) for i, pair in enumerate(kinds)] for a in others]
    send_small = [to_area(small_buf, small_rows, 3, a) for a in others]

    def to_scens(ref, target, kind):
        return [
            pltpu.make_async_remote_copy(
                src_ref=ref,
                dst_ref=target.at[d - 1],
                send_sem=scen_send.at[kind, d - 1],
                recv_sem=scen_recv.at[kind, d - 1],
                device_id={"scen": lax.rem(scen + d, n_scen)},
                device_id_type=MESH,
            )
            for d in range(1, n_scen)
        ]

    send_sums = to_scens(sums_buf, sums_in, 0)
    send_edge = to_scens(small_buf, edge_in, 1)
    turns = [lax.rem(scen + d, n_scen) for d in range(n_scen)]

    def direct(target, area, source):
        return pltpu.make_async_remote_copy(
            src_ref=small_buf.at[me],
            dst_ref=direct_buf.at[area * n_scen + source],
            send_sem=direct_send.at[target],
            recv_sem=direct_recv.at[area * n_scen + source],
            device_id={"area": 0, "scen": target},
            device_id_type=MESH,
        )

    def send_direct(act):
        for target in range(EARLY):
            copy = direct(target, me, scen)

            @pl.when(scen != target)
            def _():
                act(copy)

    def send_edges(act):
        for d in range(1, n_scen):

            @pl.when((me > 0) | (turns[d] >= EARLY))
            def _():
                act(send_edge[d - 1])


    for word in words:
        word.wait()
    for load in rows_in:
        load.wait()
    pick_row = lax.broadcasted_iota(jnp.int32, (LANES, wide), 0)
    pick_col = lax.broadcasted_iota(jnp.int32, (LANES, wide), 1)
    pick = jnp.where(pick_row - (LANES - BND) == pick_col % BND, 1.0, 0.0).astype(BF16)
    area_of = lax.broadcasted_iota(jnp.int32, (1, wide), 1) // BND
    gain = jnp.zeros((1, wide), F32)
    for j in range(MAXN):
        factor = jnp.where(j < live_ref[0], gain_ref[0, j], 0.0)
        gain = gain + jnp.where(area_of == near_ref[0, j], factor, 0.0)
    corner = dot(rows_buf[:, order - LANES :], pick)
    couple = (corner * gain).astype(BF16)
    eights = BND // 8
    high = gain.astype(BF16).astype(F32)
    part_row = lax.broadcasted_iota(jnp.int32, (8, wide), 0)
    thin = jnp.zeros((8, wide), F32)
    for q in range(eights):
        thin = thin + jnp.where(area_of == q, corner[GEN + q * 8 : GEN + q * 8 + 8], 0.0)
    gains = jnp.where(part_row < 4, high, gain - high)
    couple_buf[me] = jnp.concatenate([thin, gains], axis=0).astype(BF16)

    place = lax.broadcasted_iota(jnp.int32, (1, order), 1)
    gone = (place >= GEN) & (place < order - BND) & (place - GEN >= inner_ref[0])
    keep = jnp.where(gone, 0.0, 1.0).astype(BF16)
    matrix = rows_buf[...] * keep
    lane = lax.broadcasted_iota(jnp.int32, (1, LANES), 1)
    hour_row = lax.broadcasted_iota(jnp.int32, (hours, LANES), 0)
    hour_col = lax.broadcasted_iota(jnp.int32, (hours, LANES), 1)
    same_hour = jnp.where(hour_row == hour_col % hours, 1.0, 0.0).astype(BF16)
    fold_row = lax.broadcasted_iota(jnp.int32, (LANES, LANES), 0)
    fold_col = lax.broadcasted_iota(jnp.int32, (LANES, LANES), 1)
    fold = jnp.where(fold_row % hours == fold_col % hours, 1.0, 0.0).astype(BF16)
    fold2 = jnp.concatenate([fold, fold], axis=0)
    mean_in.wait()
    level = lax.dot_general(
        matrix, mean_buf[...], (((1,), (1,)), ((), ())), preferred_element_type=F32
    )
    level = dot(halves(level, 1), jnp.concatenate([same_hour, same_hour], axis=0))
    scen_of = lax.broadcasted_iota(jnp.int32, (1, columns), 1) // hours
    weight = jnp.zeros((1, columns), F32)
    total = jnp.float32(0.0)
    for s in range(scen_here):
        weight = jnp.where(scen_of == s, raw_ref[s], weight)
        total = total + raw_ref[s]

    def squeeze(x):
        x = x * weight
        out = x[:, :LANES]
        for k in range(1, columns // LANES):
            out = out + x[:, k * LANES : (k + 1) * LANES]
        return out

    def pack(x):
        step = x.shape[0] // groups
        out = x[:step] * spot[0]
        for k in range(1, groups):
            out = out + x[k * step : (k + 1) * step] * spot[k]
        return out

    prior_in.wait()
    old = squeeze(prior_buf[mine, :].astype(F32))
    states = []
    for load, part in zip(spread_in, parts):
        load.wait()
        states.append(
            dot(matrix, spread_buf[:, part]) + jnp.concatenate([level] * (width // LANES), axis=1)
        )
    state = jnp.concatenate(states, axis=1)

    far = (me + n_area - 1) // n_area
    late = (scen + n_scen - EARLY) // n_scen
    pl.semaphore_wait(barrier, n_area + n_scen - 2 + far * (EARLY - 1 + late))
    for some in bulk:
        some[1].start()
    spot = [jnp.where(lane // hours == k, 1.0, 0.0) for k in range(groups)]
    folded = jnp.concatenate([squeeze(state[GEN:]), old], axis=0)
    small_buf[me] = pack(dot(folded.astype(BF16), fold)).astype(BF16)

    send_direct(lambda copy: copy.start())
    for copy in send_small:
        copy.start()

    base_buf[mine, :] = state[GEN:].astype(BF16)

    odd = (me > 0) & (scen == 1)
    even = (me > 0) & (scen == 0)
    held = (me == n_area - 1) & (scen < EARLY)
    bulk[0][0].start()

    @pl.when(jnp.logical_not(odd))
    def _():
        bulk[0][2].start()

    for k in range(1, n_area - 1):

        @pl.when(k >= me)
        def _():
            for copy in bulk[k][::2]:
                copy.start()

    for k in range(1, n_area - 1):

        @pl.when((k < me) & jnp.logical_not(held))
        def _():
            bulk[k][0].start()

    gen_rows = GEN // groups
    folded = dot(halves(squeeze(state[:GEN]), 1), fold2)
    sums = jnp.concatenate([pack(folded), jnp.full((8, LANES), total, F32)], axis=0)
    sums_buf[...] = sums
    for copy in send_sums:
        copy.start()

    @pl.when(odd)
    def _():
        pl.semaphore_wait(turn_sem, 1)
        bulk[0][2].start()

    for copy in bulk[0][:2]:
        copy.wait_send()

    @pl.when(even)
    def _():
        pl.semaphore_signal(
            turn_sem, inc=1, device_id={"scen": scen + 1}, device_id_type=MESH
        )

    for k in range(1, n_area - 1):

        @pl.when((k < me) & held)
        def _():
            bulk[k][0].start()

        @pl.when(k < me)
        def _():
            bulk[k][2].start()

    arrived(small_buf, small_rows, 3)
    send_edges(lambda copy: copy.start())

    arrived(prior_buf, tie_rows, 0)
    arrived(couple_buf, small_rows, 1)
    prior = prior_buf[...]
    thin = couple_buf[...].astype(F32)
    slots = [jnp.where(lane // BND == q, 1.0, 0.0) for q in range(eights)]
    couples = jnp.concatenate(
        [thin[b, :8, :LANES] * slots[q] for b in range(n_area) for q in range(eights)], axis=0
    )
    tie_row = lax.broadcasted_iota(jnp.int32, (LANES, wide), 0)
    same_tie = jnp.where(tie_row % BND == pick_col % BND, 1.0, 0.0).astype(BF16)
    gains = jnp.concatenate(
        [jnp.broadcast_to(thin[b, 8:9] + thin[b, 12:13], (BND, wide)) for b in range(n_area)],
        axis=0,
    )
    couples = (dot(couples.astype(BF16), same_tie) * gains).astype(BF16)
    first = state[:GEN] + dot(couple[:GEN], prior)
    edge = dot(couples, prior).astype(BF16)
    gen_part = matrix[:, :GEN]
    later = state - penalty * dot(gen_part, first.astype(BF16)) + dot(couple, edge)

    for copy in send_sums:
        copy.wait_recv()
    for d in range(1, n_scen):
        sums = sums + sums_in[d - 1]
    scale = 1.0 / sums[gen_rows:]
    means = sums[:gen_rows] * jnp.concatenate([scale] * (gen_rows // 8), axis=0)
    gen_mean = jnp.concatenate([means[:gen_rows] * spot[k] for k in range(groups)], axis=0)
    gen_mean = dot(halves(gen_mean, 1), fold2)
    total_buf[...] = small_buf[...].astype(F32).reshape(total_buf.shape)

    @pl.when(lead)
    def _():
        for area in range(n_area):
            rows_of = slice(area * 8, (area + 1) * 8)
            for d in range(1, n_scen):
                direct(0, area, turns[d]).wait_recv()
                total_buf[rows_of] += direct_buf[area * n_scen + turns[d]].astype(F32)

    @pl.when(jnp.logical_not(lead))
    def _():
        for copy in send_edge:
            copy.wait_recv()
        for d in range(1, n_scen):
            total_buf[...] += edge_in[d - 1].astype(F32).reshape(total_buf.shape)

    small = total_buf[...]
    small = small * jnp.concatenate([scale] * n_area, axis=0)
    half = groups // 2
    edges = jnp.concatenate(
        [
            small[b * 8 : (b + 1) * 8] * spot[k + first_k]
            for first_k in (0, half)
            for b in range(n_area)
            for k in range(half)
        ],
        axis=0,
    )
    edges = dot(edges.astype(BF16), fold)
    prior_mean = edges[wide:].astype(BF16)
    edge_mean = (edges[:wide] + dot(couples, prior_mean)).astype(BF16)
    mean1 = gen_mean + dot(couple[:GEN], prior_mean)
    slot = lax.broadcasted_iota(jnp.int32, (GEN, LANES), 0)
    alive = jnp.where(slot < plants_ref[0], 1.0, 0.0)
    commit1 = jnp.clip(mean1, 0.0, 1.0) * alive
    both = jnp.concatenate([gen_part, gen_part], axis=1)
    mean2 = (
        gen_mean
        + penalty * dot(both[:GEN], halves(2.0 * commit1 - mean1, 0))
        + dot(couple[:GEN], edge_mean)
    )
    commit2 = jnp.clip(mean2, 0.0, 1.0) * alive
    push = dot(both, halves((2.0 * penalty) * commit1, 0))
    times = columns // LANES
    drop = jnp.concatenate([push[:GEN] - commit1 - commit2] * times, axis=1) + first
    commit_ref[0] = commit2.T[:hours]

    arrived(base_buf, tie_rows, 2)
    state2 = later + dot(couple, base_buf[...])
    dual_ref[0] = state2[:GEN] + drop
    bound_ref[0] = state2[GEN:] + jnp.concatenate([push[GEN:]] * times, axis=1)

    for copy in sum(bulk[1:], send_small + send_sums + bulk[0][2:]):
        copy.wait_send()
    send_direct(lambda copy: copy.wait_send())
    send_edges(lambda copy: copy.wait_send())


def place(*refs):
    count = (len(refs) - 1) // 2
    sems = refs[-1]
    copies = [
        pltpu.make_async_copy(refs[i], refs[count + i], sems.at[i]) for i in range(count)
    ]
    for copy in copies:
        copy.start()
    for copy in copies:
        copy.wait()


def solution(mesh):
    n_area, n_scen = mesh.shape["area"], mesh.shape["scen"]

    def body(matrix, mean, spread, raw, prior, near, live, gain, plants, inner):
        order, columns, hours = matrix.shape[2], spread.shape[2], mean.shape[2]
        hbm = pl.BlockSpec(memory_space=pltpu.HBM)
        vmem = pl.BlockSpec(memory_space=pltpu.VMEM)
        rows = GEN + BND
        wide = n_area * BND
        packed = GEN * hours // LANES + 8
        results = pl.pallas_call(
            functools.partial(kernel, n_area, n_scen),
            out_shape=(
                pltpu.VMEM((1, hours, GEN), F32),
                pltpu.VMEM((1, GEN, columns), F32),
                pltpu.VMEM((1, BND, columns), F32),
            ),
            in_specs=[hbm] * 10,
            out_specs=(vmem,) * 3,
            scratch_shapes=[
                pltpu.SMEM(raw.shape, raw.dtype),
                pltpu.SMEM(near.shape, near.dtype),
                pltpu.SMEM(live.shape, live.dtype),
                pltpu.SMEM(gain.shape, gain.dtype),
                pltpu.SMEM(plants.shape, plants.dtype),
                pltpu.SMEM(inner.shape, inner.dtype),
                pltpu.VMEM((rows, order), BF16),
                pltpu.VMEM((hours, order), BF16),
                pltpu.VMEM((order, columns), BF16),
                pltpu.VMEM((wide, columns), BF16),
                pltpu.VMEM((n_area, 16, wide), BF16),
                pltpu.VMEM((wide, columns), BF16),
                pltpu.VMEM((packed, LANES), F32),
                pltpu.VMEM((n_scen - 1, packed, LANES), F32),
                pltpu.VMEM((n_area, 8, LANES), BF16),
                pltpu.VMEM((n_scen - 1, n_area, 8, LANES), BF16),
                pltpu.VMEM((n_area * n_scen, 8, LANES), BF16),
                pltpu.VMEM((n_area * 8, LANES), F32),
                pltpu.SemaphoreType.DMA((4 + CHUNKS,)),
                pltpu.SemaphoreType.DMA((6,)),
                pltpu.SemaphoreType.DMA((4, n_area)),
                pltpu.SemaphoreType.DMA((4, n_area)),
                pltpu.SemaphoreType.DMA((2, n_scen - 1)),
                pltpu.SemaphoreType.DMA((2, n_scen - 1)),
                pltpu.SemaphoreType.DMA((EARLY,)),
                pltpu.SemaphoreType.DMA((n_area * n_scen,)),
                pltpu.SemaphoreType.REGULAR,
            ],
            compiler_params=pltpu.CompilerParams(
                collective_id=0, has_side_effects=True, vmem_limit_bytes=67043328 - 360 * 2**10
            ),
        )(
            raw,
            near,
            live,
            gain,
            plants,
            inner,
            matrix,
            jnp.swapaxes(mean, 1, 2),
            spread,
            prior,
        )
        commitment, dual, boundary = pl.pallas_call(
            place,
            out_shape=tuple(jax.ShapeDtypeStruct(x.shape, x.dtype) for x in results),
            in_specs=(vmem,) * 3,
            out_specs=(hbm,) * 3,
            scratch_shapes=[pltpu.SemaphoreType.DMA((3,))],
            compiler_params=pltpu.CompilerParams(vmem_limit_bytes=4 * 2**20),
        )(*results)
        return jnp.swapaxes(commitment, 1, 2), dual, boundary

    return jax.shard_map(
        body,
        mesh=mesh,
        in_specs=(
            P(("groups", "area"), None, None),
            P(("groups", "area"), None, None),
            P(("groups", "area"), None, "scen"),
            P(("groups", "scen")),
            P(("groups", "area"), None, "scen"),
            P(("groups", "area"), None),
            P(("groups", "area")),
            P(("groups", "area"), None),
            P(("groups", "area")),
            P(("groups", "area")),
        ),
        out_specs=(
            P(("groups", "area"), None, None),
            P(("groups", "area"), None, "scen"),
            P(("groups", "area"), None, "scen"),
        ),
        check_vma=False,
    )
```
